512 devices in a mesh: dp: 8 (over z_lo), expert: 8 (over x, z_hi), tensor: 8 (over y, core).
Axes of the slice: x: 4, y: 4, z: 16 (z_hi: 2, z_lo: 8; z = z_hi * 8 + z_lo), core: 2. Of those that a mesh axis runs over, the one named last changes fastest.
Arguments:
- tokens: bfloat16 [4096, 3072], P(('dp', 'expert', 'tensor')), parts along dimension 0, may hold values from -6 to 6
- expert_ids: int32 [4096, 2], P(('dp', 'expert', 'tensor')), parts along dimension 0, may hold values from 0 to 7, all different within a row; in each aligned block of 8 rows (0 to 7, 8 to 15, ...) at most 4 rows name the same one
- gate_weights: float32 [4096, 2], P(('dp', 'expert', 'tensor')), parts along dimension 0, may hold values from 0.2 to 1
- gate_proj: bfloat16 [8, 3072, 8192], P('expert', None, 'tensor'), may hold values from -0.109375 to 0.109375
- up_proj: bfloat16 [8, 3072, 8192], P('expert', None, 'tensor'), may hold values from -0.109375 to 0.109375
- down_proj: bfloat16 [8, 8192, 3072], P('expert', 'tensor'), may hold values from -0.0625 to 0.0625
Outputs:
- mixture: bfloat16 [4096, 3072], P(('dp', 'expert', 'tensor')), parts along dimension 0
The draws below stay inside these ranges and needn't reach their ends.
There are 8 independent parts, one for each index of `dp`. The reference program is written for one: setup_inputs(seed, part) draws one part's arguments, and reference() takes and returns one part's arrays. A program takes and returns all parts, laid end to end along the dimension named above; an argument that names none is the same for every part. Nothing has to cross between parts.
Inputs may be any that keep to these rules, and one draw needn't show every extreme that they name: `expert_ids`: each token names two different experts; no expert is named by more than 4 tokens of one device (aligned blocks of 8 rows), and some blocks reach this bound.
All inputs are finite; a program needn't handle non-finite values.
Results may differ from the reference program's by a relative error of at most 0.015.
Values may be sent and summed in bfloat16 or wider, within the bound.
No kernel may reach another device: no remote copies, remote signals or barrier semaphores. Data moves between devices by JAX's collectives and lax.ppermute only.
A program may use at most 64 MiB of HBM per device.

```python
import math
import jax
import jax.numpy as jnp
import numpy as np
from jax import lax

D = 3072
FF = 8192
TOK_DEV = 8
EXPERTS = 8
TOKENS = 512
CAP = 4
N_TENSOR = 8


def levels(key, extent, cuts, low, top_value):
    def one(dim, shards_of):
        draws = jax.random.uniform(jax.random.fold_in(jax.random.fold_in(key, 6), dim), (shards_of,), jnp.float32, low / len(cuts), top_value / len(cuts))
        return jnp.repeat(jnp.exp(draws), extent[dim] // shards_of).reshape((-1,) + (1,) * (len(extent) - dim - 1))

    level = one(*cuts[0])
    for cut in cuts[1:]:
        level = level * one(*cut)
    return level


def assign_block(key, own, number, rows, count, top, most, skew):
    order = jax.random.permutation(key, count)
    packed, usual = shares(count, rows * top, most, skew, True), shares(count, rows * top, most, skew, False)
    places = jnp.arange(count)

    def named(lengths, rotation):
        used = int((lengths > 0).sum())
        fixed = max(1, used // 4)
        moved = fixed + (places - fixed + rotation * (used - fixed)) % max(1, count - fixed)
        return jnp.zeros((count,), jnp.int32).at[order[jnp.where(places < fixed, places, moved)]].set(jnp.asarray(lengths, jnp.int32))

    lengths = jnp.where(number % 4 == 0, named(packed, number // 4), named(usual, number - number // 4 - 1))
    mixed = jax.random.permutation(jax.random.fold_in(own, 3), count)
    donor, taker = mixed[0:count // 2 * 2:2], mixed[1:count // 2 * 2:2]
    margin = jnp.minimum(lengths[donor] - 1, most - lengths[taker]) // 2
    margin = jnp.where((donor == order[0]) | (taker == order[0]) | (lengths[taker] == 0), 0, jnp.maximum(margin, 0))
    moved = jax.random.randint(jax.random.fold_in(own, 4), (count // 2,), 0, 1 << 20) % (margin + 1)
    lengths = lengths.at[donor].add(-moved).at[taker].add(moved)
    items = jnp.searchsorted(jnp.cumsum(lengths), jnp.arange(rows * top), side="right").astype(jnp.int32)
    grid = items.reshape(top, rows).T
    grid = grid[jax.random.permutation(jax.random.fold_in(own, 1), rows)]
    rotation = jax.random.randint(jax.random.fold_in(own, 2), (rows, 1), 0, top)
    return jnp.take_along_axis(grid, (jnp.arange(top)[None, :] + rotation) % top, axis=1)


def shares(count, total, limit, lean, full):
    portions = [(1 << 20) // math.isqrt(rank ** lean) + 1 for rank in range(1, count + 1)]
    largest = limit if full else min(limit, max(-(-total // count), total * portions[0] // sum(portions)))
    least = 1 if total - largest >= count - 1 else 0
    holding, spare = [largest] + [least] * (count - 1), total - largest - least * (count - 1)
    while spare > 0:
        candidates = [i for i in range(1, count) if holding[i] < largest] or [i for i in range(1, count) if holding[i] < limit]
        whole, budget = sum([portions[i] for i in candidates]), spare
        for i in candidates:
            more = min(limit - holding[i], max(1, budget * portions[i] // whole), spare)
            holding[i] = holding[i] + more
            spare = spare - more
    return np.array(holding)


def scatter_about(stream_key, extent, scale, limit, pieces=(), kind=jnp.bfloat16):
    result = jax.random.normal(stream_key, extent, jnp.float32) * scale
    if len(pieces) > 0:
        result = levels(stream_key, extent, pieces, -0.22, 0.18) * result
    return jnp.clip(result, min=-limit, max=limit).astype(kind)


def setup_inputs(seed: int = 0, part: int = 0) -> dict:
    arg_keys = jax.random.split(jax.random.key(seed), 7)
    own_keys = jax.random.split(jax.random.fold_in(arg_keys[6], part), 7)
    tokens = scatter_about(own_keys[0], (TOKENS, D), 1.0, 6.0, ((0, 64),))
    expert_ids_keys = jax.random.split(jax.random.fold_in(own_keys[1], 1), TOKENS // TOK_DEV)
    expert_ids_turns = jax.random.permutation(jax.random.fold_in(own_keys[1], 3), TOKENS // TOK_DEV)
    expert_ids = jax.vmap(lambda own, number: assign_block(jax.random.fold_in(own_keys[1], 2), own, number, TOK_DEV, EXPERTS, 2, CAP, 2))(expert_ids_keys, expert_ids_turns).reshape((TOKENS, 2))
    gate_weights = jnp.clip(0.2 + 0.8 * jax.random.uniform(own_keys[2], (TOKENS, 2), jnp.float32) ** levels(own_keys[2], (TOKENS, 2), ((0, 64),), -0.2, 0.2), 0.2, 1.0)
    gate_proj = scatter_about(arg_keys[3], (EXPERTS, D, FF), D ** -0.5, 0.109375, ((0, 8), (2, 8)))
    up_proj = scatter_about(arg_keys[4], (EXPERTS, D, FF), D ** -0.5, 0.109375, ((0, 8), (2, 8)))
    down_proj = scatter_about(arg_keys[5], (EXPERTS, FF, D), FF ** -0.5, 0.0625, ((0, 8), (1, 8)))
    return {"tokens": tokens, "expert_ids": expert_ids, "gate_weights": gate_weights, "gate_proj": gate_proj, "up_proj": up_proj, "down_proj": down_proj}


def expert_rows(rows, w_gate, w_up, w_down):
    gate = jnp.dot(rows, w_gate, preferred_element_type=jnp.float32)
    upward = jnp.dot(rows, w_up, preferred_element_type=jnp.float32)
    hidden = (jax.nn.silu(gate) * upward).astype(jnp.bfloat16)
    group = FF // N_TENSOR
    total = jnp.zeros((rows.shape[0], D), jnp.float32)
    for index in range(N_TENSOR):
        part_hidden = hidden[:, index * group:(index + 1) * group]
        part_down = w_down[index * group:(index + 1) * group]
        partial_value = jnp.dot(part_hidden, part_down, preferred_element_type=jnp.float32).astype(jnp.bfloat16)
        total = total + partial_value.astype(jnp.float32)
    return total.astype(jnp.bfloat16)


def reference(tokens, expert_ids, gate_weights, gate_proj, up_proj, down_proj):
    blocks = TOKENS // TOK_DEV
    ids = expert_ids.reshape(blocks, 2 * TOK_DEV).astype(jnp.int32)
    onehot = (ids[:, :, None] == jnp.arange(EXPERTS, dtype=jnp.int32)[None, None, :]).astype(jnp.int32)
    earlier = jnp.cumsum(onehot, axis=1) - onehot
    slots = jnp.sum(onehot * earlier, axis=2)
    target = ids * CAP + slots
    placed = (target[:, :, None] == jnp.arange(EXPERTS * CAP, dtype=jnp.int32)[None, None, :]).astype(jnp.float32)
    doubled = jnp.repeat(tokens.reshape(blocks, TOK_DEV, D).astype(jnp.float32), 2, axis=1)
    buffer = jnp.einsum("brs,brd->bsd", placed, doubled, precision=lax.Precision.HIGHEST).astype(jnp.bfloat16)
    per_expert = buffer.reshape(blocks, EXPERTS, CAP, D).transpose(1, 0, 2, 3).reshape(EXPERTS, blocks * CAP, D)
    outputs = lax.map(lambda items: expert_rows(items[0], items[1], items[2], items[3]),
                      (per_expert, gate_proj, up_proj, down_proj))
    back = outputs.reshape(EXPERTS, blocks, CAP, D).transpose(1, 0, 2, 3).reshape(blocks, EXPERTS * CAP, D)
    weights = placed * gate_weights.reshape(blocks, 2 * TOK_DEV)[:, :, None]
    contrib = jnp.einsum("brs,bsd->brd", weights, back.astype(jnp.float32), precision=lax.Precision.HIGHEST)
    return contrib.reshape(blocks, TOK_DEV, 2, D).sum(axis=2).reshape(TOKENS, D).astype(jnp.bfloat16)
```

```python
import functools

import jax
import jax.numpy as jnp
from jax import lax
from jax.experimental import pallas as pl
from jax.experimental.pallas import tpu as pltpu
from jax.sharding import Mesh, PartitionSpec as P

X, ZH, Y, CORE = 4, 2, 4, 2
SLOTS = 4
META = 128
BF16, F32 = jnp.bfloat16, jnp.float32
VMEM = pltpu.MemorySpace.VMEM
SMEM = pltpu.MemorySpace.SMEM


def dot(a, b, contract=((1,), (0,))):
    return lax.dot_general(a, b, (contract, ((), ())), preferred_element_type=F32)


def iota(shape, dim):
    return lax.broadcasted_iota(jnp.int32, shape, dim)


def pack_kernel(tok_ref, ids_ref, gw_ref, out_ref, meta_ref):
    rows, width = tok_ref.shape
    out_ref[:, :width] = tok_ref[...]
    w = gw_ref[...]
    high = w.astype(BF16).astype(F32)
    mid = (w - high).astype(BF16).astype(F32)
    meta_ref[...] = jnp.zeros(meta_ref.shape, F32)
    meta_ref[0:2, 0:rows] = ids_ref[...].astype(F32)
    meta_ref[2:4, 0:rows] = high
    meta_ref[4:6, 0:rows] = mid
    meta_ref[6:8, 0:rows] = w - high - mid
    out_ref[:, width:] = meta_ref[...].astype(BF16)


def packed(tokens, ids, gate_weights):
    rows, width = tokens.shape
    return pl.pallas_call(
        pack_kernel,
        out_shape=jax.ShapeDtypeStruct((rows, width + META), BF16),
        scratch_shapes=[pltpu.VMEM((8, META), F32)],
        name="pack",
    )(tokens, ids.T, gate_weights.T)


def placement(meta, zh, block):
    rows = 8
    meta = meta.astype(F32)
    r = iota((X * 2 * SLOTS, rows), 0)
    expert = ((r // (2 * SLOTS)) * ZH + zh).astype(F32)
    named = jnp.where((meta[0:1, :rows] == expert) | (meta[1:2, :rows] == expert), 1.0, 0.0)
    before = jnp.where(iota((rows, rows), 0) < iota((rows, rows), 1), 1.0, 0.0)
    rank = dot(named.astype(BF16), before.astype(BF16))
    mine = (r // SLOTS) % 2 == block
    return jnp.where(mine & (named > 0.5) & (rank == (r % SLOTS).astype(F32)), 1.0, 0.0).astype(BF16)


def place_kernel(zh_ref, own_ref, other_ref, out_ref):
    width = out_ref.shape[-1]
    zh = zh_ref[0]
    slots = dot(placement(own_ref[:, width:], zh, 0), own_ref[:, :width])
    slots = slots + dot(placement(other_ref[:, width:], zh, 1), other_ref[:, :width])
    slots = slots.astype(BF16)
    for x in range(X):
        for y in range(Y):
            out_ref[x * Y + y] = slots[x * 2 * SLOTS : (x + 1) * 2 * SLOTS]


def placed(zh, own, other):
    width = own.shape[1] - META
    return pl.pallas_call(
        place_kernel,
        out_shape=jax.ShapeDtypeStruct((X * Y, 2 * SLOTS, width), BF16),
        in_specs=[pl.BlockSpec(memory_space=SMEM), pl.BlockSpec(memory_space=VMEM), pl.BlockSpec(memory_space=VMEM)],
        name="place",
    )(zh, own, other)


def ffn_kernel(a_ref, b_ref, wg_ref, wu_ref, wd_ref, pa_ref, pb_ref, rows_ref, acc_ref):
    step = pl.program_id(0)
    half = a_ref.shape[0]

    @pl.when(step == 0)
    def _():
        rows_ref[:half] = a_ref[...]
        rows_ref[half:] = b_ref[...]

    rows = rows_ref[...]
    gate = dot(rows, wg_ref[0])
    up = dot(rows, wu_ref[0])
    hidden = (gate / (1.0 + jnp.exp(-gate)) * up).astype(BF16)
    part = dot(hidden, wd_ref[0])

    @pl.when(step == 0)
    def _():
        acc_ref[...] = part

    @pl.when(step > 0)
    def _():
        acc_ref[...] += part

    @pl.when(step == pl.num_programs(0) - 1)
    def _():
        pa_ref[...] = acc_ref[:half]
        pb_ref[...] = acc_ref[half:].astype(BF16)


def ffn(a, b, wg, wu, wd, block=256):
    half, width = a.shape
    hidden = wg.shape[2]
    whole = pl.BlockSpec((half, width), lambda i: (0, 0))
    return pl.pallas_call(
        ffn_kernel,
        out_shape=(jax.ShapeDtypeStruct((half, width), F32), jax.ShapeDtypeStruct((half, width), BF16)),
        grid=(hidden // block,),
        in_specs=[
            whole,
            whole,
            pl.BlockSpec((1, width, block), lambda i: (0, 0, i)),
            pl.BlockSpec((1, width, block), lambda i: (0, 0, i)),
            pl.BlockSpec((1, block, width), lambda i: (0, i, 0)),
        ],
        out_specs=(whole, whole),
        scratch_shapes=[pltpu.VMEM((2 * half, width), BF16), pltpu.VMEM((2 * half, width), F32)],
        compiler_params=pltpu.CompilerParams(vmem_limit_bytes=48 * 2**20),
        name="ffn",
    )(a, b, wg, wu, wd)


def mixing(meta, zh, block):
    rows = 8
    eye = jnp.where(iota((8, 8), 0) == iota((8, 8), 1), 1.0, 0.0).astype(BF16)
    fields = dot(eye, meta[:, :rows], ((1,), (1,)))
    lanes = X * Y * 2 * SLOTS
    r = iota((rows, lanes), 1)
    expert = ((r // (Y * 2 * SLOTS)) * ZH + zh).astype(F32)
    first = fields[:, 0:1] == expert
    second = fields[:, 1:2] == expert
    named = jnp.where(first | second, 1.0, 0.0)
    before = jnp.where(iota((rows, rows), 1) < iota((rows, rows), 0), 1.0, 0.0)
    rank = dot(before.astype(BF16), named.astype(BF16))
    w0 = fields[:, 2:3] + fields[:, 4:5] + fields[:, 6:7]
    w1 = fields[:, 3:4] + fields[:, 5:6] + fields[:, 7:8]
    mine = (r // SLOTS) % 2 == block
    weight = jnp.where(first, w0, jnp.where(second, w1, 0.0))
    return jnp.where(mine & (rank == (r % SLOTS).astype(F32)), weight, 0.0)


def mixed(weights, rows):
    high = weights.astype(BF16)
    rest = weights - high.astype(F32)
    mid = rest.astype(BF16)
    low = (rest - mid.astype(F32)).astype(BF16)
    return dot(high, rows) + dot(mid, rows) + dot(low, rows)


def combine_kernel(zh_ref, rows_ref, own_ref, other_ref, keep_ref, send_ref):
    zh = zh_ref[0]
    rows = rows_ref[...]
    keep_ref[...] = mixed(mixing(own_ref[...], zh, 0), rows)
    send_ref[...] = mixed(mixing(other_ref[...], zh, 1), rows).astype(BF16)


def combined(zh, rows, own, other):
    width = rows.shape[1]
    meta = pl.BlockSpec((8, META), lambda i: (0, width // META))
    tokens = pl.BlockSpec((8, width), lambda i: (0, 0))
    return pl.pallas_call(
        combine_kernel,
        grid=(1,),
        out_shape=(jax.ShapeDtypeStruct((8, width), F32), jax.ShapeDtypeStruct((8, width), BF16)),
        in_specs=[pl.BlockSpec(memory_space=SMEM), pl.BlockSpec(rows.shape, lambda i: (0, 0)), meta, meta],
        out_specs=(tokens, tokens),
        name="combine",
    )(zh, rows, own, other)


def swapped(value, axis):
    return lax.ppermute(value, axis, [(0, 1), (1, 0)])


def on_device(tokens, expert_ids, gate_weights, gate_proj, up_proj, down_proj):
    width = tokens.shape[1]
    zh = lax.axis_index("zh").astype(jnp.int32).reshape(1)
    own = packed(tokens, expert_ids, gate_weights)
    other = swapped(own, "zh")
    slots = placed(zh, own, other)
    rows = lax.all_to_all(slots, ("x", "y"), 0, 0, tiled=True).reshape(-1, width)
    core_rows = swapped(rows, "core")
    part, core_part = ffn(rows, core_rows, gate_proj, up_proj, down_proj)
    pair = (part + swapped(core_part, "core").astype(F32)).astype(BF16)
    back = lax.all_to_all(pair.reshape(slots.shape), ("x", "y"), 0, 0, tiled=True)
    keep, send = combined(zh, back.reshape(-1, width), own, other)
    return (keep + swapped(send, "zh").astype(F32)).astype(BF16)


def solution(mesh):
    dp = mesh.shape["dp"]
    fine = Mesh(mesh.devices.reshape(dp, X, ZH, Y, CORE), ("dp", "x", "zh", "y", "core"))
    every = P(("dp", "x", "zh", "y", "core"), None)
    return jax.shard_map(
        on_device,
        mesh=fine,
        in_specs=(
            every,
            every,
            every,
            P(("x", "zh"), None, ("y", "core")),
            P(("x", "zh"), None, ("y", "core")),
            P(("x", "zh"), ("y", "core"), None),
        ),
        out_specs=every,
        check_vma=False,
    )
```

```python
import functools

import jax
import jax.numpy as jnp
from jax import lax
from jax.experimental import pallas as pl
from jax.experimental.pallas import tpu as pltpu
from jax.sharding import Mesh, PartitionSpec as P

X, ZH, Y, CORE = 4, 2, 4, 2
SLOTS = 4
META = 128
BF16, F32 = jnp.bfloat16, jnp.float32
VMEM = pltpu.MemorySpace.VMEM
SMEM = pltpu.MemorySpace.SMEM


def dot(a, b, contract=((1,), (0,))):
    return lax.dot_general(a, b, (contract, ((), ())), preferred_element_type=F32)


def iota(shape, dim):
    return lax.broadcasted_iota(jnp.int32, shape, dim)


def call(kernel, outs, args, name, scratch=(), limit=4 * 2**20):
    specs = [pl.BlockSpec(memory_space=SMEM if a.size == 1 else VMEM) for a in args]
    args = [a if a.size == 1 else pltpu.with_memory_space_constraint(a, VMEM) for a in args]
    return pl.pallas_call(
        kernel,
        out_shape=tuple(VMEM(shape, dtype) for shape, dtype in outs),
        in_specs=specs,
        out_specs=tuple(pl.BlockSpec(memory_space=VMEM) for _ in outs),
        scratch_shapes=scratch,
        compiler_params=pltpu.CompilerParams(vmem_limit_bytes=limit),
        name=name,
    )(*args)


def in_hbm(*arrays):
    return [pltpu.with_memory_space_constraint(a, pltpu.MemorySpace.HBM) for a in arrays]


def pack_kernel(tok_ref, ids_ref, gw_ref, out_ref, meta_ref):
    rows, width = tok_ref.shape
    out_ref[:, :width] = tok_ref[...]
    w = gw_ref[...]
    high = w.astype(BF16).astype(F32)
    mid = (w - high).astype(BF16).astype(F32)
    meta_ref[...] = jnp.zeros(meta_ref.shape, F32)
    meta_ref[0:2, 0:rows] = ids_ref[...].astype(F32)
    meta_ref[2:4, 0:rows] = high
    meta_ref[4:6, 0:rows] = mid
    meta_ref[6:8, 0:rows] = w - high - mid
    out_ref[:, width:] = meta_ref[...].astype(BF16)


def packed(tokens, ids, gate_weights):
    rows, width = tokens.shape
    return pl.pallas_call(
        pack_kernel,
        out_shape=VMEM((rows, width + META), BF16),
        out_specs=pl.BlockSpec(memory_space=VMEM),
        scratch_shapes=[pltpu.VMEM((8, META), F32)],
        compiler_params=pltpu.CompilerParams(vmem_limit_bytes=2**20),
        name="pack",
    )(*in_hbm(tokens, ids.T, gate_weights.T))


def placement(meta, zh, block):
    rows = 8
    meta = meta.astype(F32)
    r = iota((X * 2 * SLOTS, rows), 0)
    expert = ((r // (2 * SLOTS)) * ZH + zh).astype(F32)
    named = jnp.where((meta[0:1, :rows] == expert) | (meta[1:2, :rows] == expert), 1.0, 0.0)
    before = jnp.where(iota((rows, rows), 0) < iota((rows, rows), 1), 1.0, 0.0)
    rank = dot(named.astype(BF16), before.astype(BF16))
    mine = (r // SLOTS) % 2 == block
    return jnp.where(mine & (named > 0.5) & (rank == (r % SLOTS).astype(F32)), 1.0, 0.0).astype(BF16)


def place_kernel(zh_ref, own_ref, other_ref, out_ref, both_ref):
    width = out_ref.shape[-1]
    zh = zh_ref[0]
    both_ref[0:8] = own_ref[:, :width]
    both_ref[8:16] = other_ref[:, :width]
    places = [placement(own_ref[:, width:], zh, 0), placement(other_ref[:, width:], zh, 1)]
    slots = dot(jnp.concatenate(places, axis=1), both_ref[...]).astype(BF16)
    for x in range(X):
        for y in range(Y):
            out_ref[x * Y + y] = slots[x * 2 * SLOTS : (x + 1) * 2 * SLOTS]


def placed(zh, own, other):
    width = own.shape[1] - META
    outs = [((X * Y, 2 * SLOTS, width), BF16)]
    return call(place_kernel, outs, (zh, own, other), "place", [pltpu.VMEM((16, width), BF16)])[0]


def ffn_kernel(a_ref, b_ref, wg_ref, wu_ref, wd_ref, pa_ref, pb_ref, rows_ref, hidden_ref):
    half, width = a_ref.shape
    rows_ref[:half] = a_ref[...]
    rows_ref[half:] = b_ref[...]
    block = 256
    for start in range(0, hidden_ref.shape[1], block):
        gate = dot(rows_ref[...], wg_ref[0, :, start : start + block])
        up = dot(rows_ref[...], wu_ref[0, :, start : start + block])
        hidden_ref[:, start : start + block] = (gate / (1.0 + jnp.exp(-gate)) * up).astype(BF16)
    for start in range(0, width, block):
        part = dot(hidden_ref[...], wd_ref[0, :, start : start + block])
        pa_ref[:, start : start + block] = part[:half]
        pb_ref[:, start : start + block] = part[half:].astype(BF16)


def ffn(a, b, wg, wu, wd):
    half, width = a.shape
    hidden = wg.shape[2]
    scratch = [pltpu.VMEM((2 * half, width), BF16), pltpu.VMEM((2 * half, hidden), BF16)]
    outs = [((half, width), F32), ((half, width), BF16)]
    return call(ffn_kernel, outs, (a, b, wg, wu, wd), "ffn", scratch, 16 * 2**20)


PIECES = 4


def load_kernel(*refs):
    sources, targets, sems = refs[1:4], refs[4:7], refs[7]
    copies = []
    for source, target in zip(sources, targets):
        rows = source.shape[1] // PIECES
        for piece in range(PIECES):
            part = pl.ds(piece * rows, rows)
            copies.append(pltpu.make_async_copy(source.at[0, part], target.at[0, part], sems.at[len(copies)]))
    for copy in copies:
        copy.start()
    for copy in copies:
        copy.wait()


def loaded(after, *weights):
    anywhere = pl.BlockSpec(memory_space=pl.ANY)
    return pl.pallas_call(
        load_kernel,
        out_shape=tuple(VMEM(w.shape, w.dtype) for w in weights),
        in_specs=[anywhere] * (1 + len(weights)),
        out_specs=tuple(pl.BlockSpec(memory_space=VMEM) for _ in weights),
        scratch_shapes=[pltpu.SemaphoreType.DMA((len(weights) * PIECES,))],
        cost_estimate=pl.CostEstimate(flops=0, transcendentals=0, bytes_accessed=2 * sum(w.size * 2 for w in weights)),
        compiler_params=pltpu.CompilerParams(vmem_limit_bytes=2**20),
        name="load",
    )(after, *in_hbm(*weights))


def mixing(meta, zh, block):
    rows = 8
    eye = jnp.where(iota((8, 8), 0) == iota((8, 8), 1), 1.0, 0.0).astype(BF16)
    fields = dot(eye, meta[:, :rows], ((1,), (1,)))
    lanes = X * Y * 2 * SLOTS
    r = iota((rows, lanes), 1)
    expert = ((r // (Y * 2 * SLOTS)) * ZH + zh).astype(F32)
    first = fields[:, 0:1] == expert
    second = fields[:, 1:2] == expert
    named = jnp.where(first | second, 1.0, 0.0)
    before = jnp.where(iota((rows, rows), 1) < iota((rows, rows), 0), 1.0, 0.0)
    rank = dot(before.astype(BF16), named.astype(BF16))
    w0 = fields[:, 2:3] + fields[:, 4:5] + fields[:, 6:7]
    w1 = fields[:, 3:4] + fields[:, 5:6] + fields[:, 7:8]
    mine = (r // SLOTS) % 2 == block
    weight = jnp.where(first, w0, jnp.where(second, w1, 0.0))
    return jnp.where(mine & (rank == (r % SLOTS).astype(F32)), weight, 0.0)


def mixed(weights, rows):
    high = weights.astype(BF16).astype(F32)
    mid = (weights - high).astype(BF16).astype(F32)
    parts = jnp.concatenate([high, mid, weights - high - mid], axis=0)
    total = dot(parts.astype(BF16), rows)
    return total[0:8] + total[8:16] + total[16:24]


def mix_kernel(zh_ref, rows_ref, packed_ref, out_ref, *, block):
    meta = packed_ref[:, rows_ref.shape[1] :]
    out_ref[...] = mixed(mixing(meta, zh_ref[0], block), rows_ref[...]).astype(out_ref.dtype)


def mix(zh, rows, source, block, dtype):
    kernel = functools.partial(mix_kernel, block=block)
    return call(kernel, [((8, rows.shape[1]), dtype)], (zh, rows, source), "mix%d" % block)[0]


def swapped(value, axis):
    return lax.ppermute(value, axis, [(0, 1), (1, 0)])


def on_device(tokens, expert_ids, gate_weights, gate_proj, up_proj, down_proj):
    width = tokens.shape[1]
    zh = lax.axis_index("zh").astype(jnp.int32).reshape(1)
    own = packed(tokens, expert_ids, gate_weights)
    other = swapped(own, "zh")
    weights = loaded(own, gate_proj, up_proj, down_proj)
    other, weights = lax.optimization_barrier((other, weights))
    slots = placed(zh, own, other)
    rows = lax.all_to_all(slots, ("x", "y"), 0, 0, tiled=True).reshape(-1, width)
    core_rows = swapped(rows, "core")
    part, core_part = ffn(rows, core_rows, *weights)
    pair = (part + swapped(core_part, "core").astype(F32)).astype(BF16)
    back = lax.all_to_all(pair.reshape(slots.shape), ("x", "y"), 0, 0, tiled=True)
    back = back.reshape(-1, width)
    arriving = swapped(mix(zh, back, other, 1, BF16), "zh")
    keep = mix(zh, back, own, 0, F32)
    return (keep + arriving.astype(F32)).astype(BF16)


def solution(mesh):
    dp = mesh.shape["dp"]
    fine = Mesh(mesh.devices.reshape(dp, X, ZH, Y, CORE), ("dp", "x", "zh", "y", "core"))
    every = P(("dp", "x", "zh", "y", "core"), None)
    return jax.shard_map(
        on_device,
        mesh=fine,
        in_specs=(
            every,
            every,
            every,
            P(("x", "zh"), None, ("y", "core")),
            P(("x", "zh"), None, ("y", "core")),
            P(("x", "zh"), ("y", "core"), None),
        ),
        out_specs=every,
        check_vma=False,
    )
```

```python
import functools

import jax
import jax.numpy as jnp
from jax import lax
from jax.experimental import pallas as pl
from jax.experimental.pallas import tpu as pltpu
from jax.sharding import Mesh, PartitionSpec as P

X, ZH, Y, CORE = 4, 2, 4, 2
SLOTS = 4
META = 128
BF16, F32 = jnp.bfloat16, jnp.float32
VMEM = pltpu.MemorySpace.VMEM
SMEM = pltpu.MemorySpace.SMEM


def dot(a, b, contract=((1,), (0,))):
    return lax.dot_general(a, b, (contract, ((), ())), preferred_element_type=F32)


def iota(shape, dim):
    return lax.broadcasted_iota(jnp.int32, shape, dim)


def call(kernel, outs, args, name, scratch=(), limit=8 * 2**20, flops=0):
    specs = [pl.BlockSpec(memory_space=SMEM if a.size == 1 else VMEM) for a in args]
    args = [a if a.size == 1 else pltpu.with_memory_space_constraint(a, VMEM) for a in args]
    return pl.pallas_call(
        kernel,
        out_shape=tuple(VMEM(shape, dtype) for shape, dtype in outs),
        in_specs=specs,
        out_specs=tuple(pl.BlockSpec(memory_space=VMEM) for _ in outs),
        scratch_shapes=scratch,
        compiler_params=pltpu.CompilerParams(vmem_limit_bytes=limit),
        cost_estimate=pl.CostEstimate(flops=flops, transcendentals=0, bytes_accessed=0) if flops else None,
        name=name,
    )(*args)


def in_hbm(*arrays):
    return [pltpu.with_memory_space_constraint(a, pltpu.MemorySpace.HBM) for a in arrays]


def pack_kernel(tok_ref, ids_ref, gw_ref, out_ref, meta_ref):
    rows, width = tok_ref.shape
    out_ref[:, :width] = tok_ref[...]
    w = gw_ref[...]
    high = w.astype(BF16).astype(F32)
    mid = (w - high).astype(BF16).astype(F32)
    meta_ref[...] = jnp.zeros(meta_ref.shape, F32)
    meta_ref[0:2, 0:rows] = ids_ref[...].astype(F32)
    meta_ref[2:4, 0:rows] = high
    meta_ref[4:6, 0:rows] = mid
    meta_ref[6:8, 0:rows] = w - high - mid
    out_ref[:, width:] = meta_ref[...].astype(BF16)


def packed(tokens, ids, gate_weights):
    rows, width = tokens.shape
    return pl.pallas_call(
        pack_kernel,
        out_shape=VMEM((rows, width + META), BF16),
        out_specs=pl.BlockSpec(memory_space=VMEM),
        scratch_shapes=[pltpu.VMEM((8, META), F32)],
        compiler_params=pltpu.CompilerParams(vmem_limit_bytes=2**20),
        name="pack",
    )(*in_hbm(tokens, ids.T, gate_weights.T))


def placement(meta, zh, block):
    rows = 8
    meta = meta.astype(F32)
    r = iota((X * 2 * SLOTS, rows), 0)
    expert = ((r // (2 * SLOTS)) * ZH + zh).astype(F32)
    named = jnp.where((meta[0:1, :rows] == expert) | (meta[1:2, :rows] == expert), 1.0, 0.0)
    before = jnp.where(iota((rows, rows), 0) < iota((rows, rows), 1), 1.0, 0.0)
    rank = dot(named.astype(BF16), before.astype(BF16))
    mine = (r // SLOTS) % 2 == block
    return jnp.where(mine & (named > 0.5) & (rank == (r % SLOTS).astype(F32)), 1.0, 0.0).astype(BF16)


def place_kernel(zh_ref, own_ref, other_ref, out_ref, both_ref):
    width = out_ref.shape[-1]
    zh = zh_ref[0]
    both_ref[0:8] = own_ref[:, :width]
    both_ref[8:16] = other_ref[:, :width]
    places = [placement(own_ref[:, width:], zh, 0), placement(other_ref[:, width:], zh, 1)]
    slots = dot(jnp.concatenate(places, axis=1), both_ref[...]).astype(BF16)
    for x in range(X):
        for y in range(Y):
            out_ref[x * Y + y] = slots[x * 2 * SLOTS : (x + 1) * 2 * SLOTS]


def placed(zh, own, other):
    width = own.shape[1] - META
    outs = [((X * Y, 2 * SLOTS, width), BF16)]
    return call(place_kernel, outs, (zh, own, other), "place", [pltpu.VMEM((16, width), BF16)])[0]


BLOCK = 256


def hidden_units(rows, wg_ref, wu_ref, out_ref):
    for start in range(0, out_ref.shape[1], BLOCK):
        gate = dot(rows, wg_ref[0, :, start : start + BLOCK])
        up = dot(rows, wu_ref[0, :, start : start + BLOCK])
        out_ref[:, start : start + BLOCK] = (gate / (1.0 + jnp.exp(-gate)) * up).astype(BF16)


def down(hidden, wd_ref, out_ref):
    for start in range(0, out_ref.shape[1], BLOCK):
        out_ref[:, start : start + BLOCK] = dot(hidden, wd_ref[0, :, start : start + BLOCK]).astype(out_ref.dtype)


def hidden_kernel(rows_ref, wg_ref, wu_ref, out_ref):
    hidden_units(rows_ref[...], wg_ref, wu_ref, out_ref)


def down_kernel(hidden_ref, wd_ref, out_ref):
    down(hidden_ref[...], wd_ref, out_ref)


def expert_kernel(rows_ref, wg_ref, wu_ref, wd_ref, out_ref, hidden_ref):
    hidden_units(rows_ref[...], wg_ref, wu_ref, hidden_ref)
    down(hidden_ref[...], wd_ref, out_ref)


PIECES = 4


def load_kernel(*refs):
    sources, targets, sems = refs[1:4], refs[4:7], refs[7]
    copies = []
    for source, target in zip(sources, targets):
        rows = source.shape[1] // PIECES
        for piece in range(PIECES):
            part = pl.ds(piece * rows, rows)
            copies.append(pltpu.make_async_copy(source.at[0, part], target.at[0, part], sems.at[len(copies)]))
    for copy in copies:
        copy.start()
    for copy in copies:
        copy.wait()


def loaded(after, *weights):
    anywhere = pl.BlockSpec(memory_space=pl.ANY)
    return pl.pallas_call(
        load_kernel,
        out_shape=tuple(VMEM(w.shape, w.dtype) for w in weights),
        in_specs=[anywhere] * (1 + len(weights)),
        out_specs=tuple(pl.BlockSpec(memory_space=VMEM) for _ in weights),
        scratch_shapes=[pltpu.SemaphoreType.DMA((len(weights) * PIECES,))],
        cost_estimate=pl.CostEstimate(flops=0, transcendentals=0, bytes_accessed=2 * sum(w.size * 2 for w in weights)),
        compiler_params=pltpu.CompilerParams(vmem_limit_bytes=2**20),
        name="load",
    )(after, *in_hbm(*weights))


def mixing(meta, zh, block):
    rows = 8
    eye = jnp.where(iota((8, 8), 0) == iota((8, 8), 1), 1.0, 0.0).astype(BF16)
    fields = dot(eye, meta[:, :rows], ((1,), (1,)))
    lanes = X * Y * 2 * SLOTS
    r = iota((rows, lanes), 1)
    expert = ((r // (Y * 2 * SLOTS)) * ZH + zh).astype(F32)
    first = fields[:, 0:1] == expert
    second = fields[:, 1:2] == expert
    named = jnp.where(first | second, 1.0, 0.0)
    before = jnp.where(iota((rows, rows), 1) < iota((rows, rows), 0), 1.0, 0.0)
    rank = dot(before.astype(BF16), named.astype(BF16))
    w0 = fields[:, 2:3] + fields[:, 4:5] + fields[:, 6:7]
    w1 = fields[:, 3:4] + fields[:, 5:6] + fields[:, 7:8]
    mine = (r // SLOTS) % 2 == block
    weight = jnp.where(first, w0, jnp.where(second, w1, 0.0))
    return jnp.where(mine & (rank == (r % SLOTS).astype(F32)), weight, 0.0)


def split(weights):
    high = weights.astype(BF16).astype(F32)
    mid = (weights - high).astype(BF16).astype(F32)
    return jnp.concatenate([high, mid, weights - high - mid], axis=0).astype(BF16)


def weights_kernel(zh_ref, own_ref, other_ref, after_ref, own_out, other_out):
    width = own_ref.shape[1] - META
    own_out[...] = split(mixing(own_ref[:, width:], zh_ref[0], 0))
    other_out[...] = split(mixing(other_ref[:, width:], zh_ref[0], 1))


def mix_kernel(weights_ref, rows_ref, out_ref):
    total = dot(weights_ref[...], rows_ref[...])
    out_ref[...] = (total[0:8] + total[8:16] + total[16:24]).astype(out_ref.dtype)


def mix(weights, rows, dtype, name):
    return call(mix_kernel, [((8, rows.shape[1]), dtype)], (weights, rows), name, flops=2 * weights.shape[0] * rows.size)[0]


def swapped(value, axis):
    return lax.ppermute(value, axis, [(0, 1), (1, 0)])


def on_device(tokens, expert_ids, gate_weights, gate_proj, up_proj, down_proj):
    width = tokens.shape[1]
    units = gate_proj.shape[2]
    zh = lax.axis_index("zh").astype(jnp.int32).reshape(1)
    own = packed(tokens, expert_ids, gate_weights)
    other = swapped(own, "zh")
    weights = loaded(own, gate_proj, up_proj, down_proj)
    other, (wg, wu, wd) = lax.optimization_barrier((other, weights))
    slots = placed(zh, own, other)
    half = slots.shape[0] * slots.shape[1]
    rows = lax.all_to_all(slots, ("x", "y"), 0, 0, tiled=True).reshape(half, width)
    core_rows = swapped(rows, "core")
    third = 2 * half * width * units
    hidden = call(hidden_kernel, [((half, units), BF16)], (rows, wg, wu), "hidden", flops=2 * third)[0]
    core_rows, hidden = lax.optimization_barrier((core_rows, hidden))
    scratch = [pltpu.VMEM((half, units), BF16)]
    core_part = call(expert_kernel, [((half, width), BF16)], (core_rows, wg, wu, wd), "expert", scratch, flops=3 * third)[0]
    arrived = swapped(core_part, "core")
    part = call(down_kernel, [((half, width), F32)], (hidden, wd), "down", flops=third)[0]
    pair = (part + arrived.astype(F32)).astype(BF16).reshape(slots.shape)
    back = lax.all_to_all(pair, ("x", "y"), 0, 0, tiled=True)
    outs = [((24, half), BF16), ((24, half), BF16)]
    own_weights, other_weights = call(weights_kernel, outs, (zh, own, other, pair), "weights", flops=2**28)
    back = back.reshape(half, width)
    arriving = swapped(mix(other_weights, back, BF16, "mix_other"), "zh")
    keep = mix(own_weights, back, F32, "mix_own")
    return (keep + arriving.astype(F32)).astype(BF16)


def solution(mesh):
    dp = mesh.shape["dp"]
    fine = Mesh(mesh.devices.reshape(dp, X, ZH, Y, CORE), ("dp", "x", "zh", "y", "core"))
    every = P(("dp", "x", "zh", "y", "core"), None)
    return jax.shard_map(
        on_device,
        mesh=fine,
        in_specs=(
            every,
            every,
            every,
            P(("x", "zh"), None, ("y", "core")),
            P(("x", "zh"), None, ("y", "core")),
            P(("x", "zh"), ("y", "core"), None),
        ),
        out_specs=every,
        check_vma=False,
    )
```

```python
import functools

import jax
import jax.numpy as jnp
from jax import lax
from jax.experimental import pallas as pl
from jax.experimental.pallas import tpu as pltpu
from jax.sharding import Mesh, PartitionSpec as P

X, ZH, Y, CORE = 4, 2, 4, 2
SLOTS = 4
META = 128
BF16, F32 = jnp.bfloat16, jnp.float32
VMEM = pltpu.MemorySpace.VMEM
SMEM = pltpu.MemorySpace.SMEM


def dot(a, b, contract=((1,), (0,))):
    return lax.dot_general(a, b, (contract, ((), ())), preferred_element_type=F32)


def iota(shape, dim):
    return lax.broadcasted_iota(jnp.int32, shape, dim)


def call(kernel, outs, args, name, scratch=(), limit=8 * 2**20, flops=0):
    specs = [pl.BlockSpec(memory_space=SMEM if a.size == 1 else VMEM) for a in args]
    args = [a if a.size == 1 else pltpu.with_memory_space_constraint(a, VMEM) for a in args]
    return pl.pallas_call(
        kernel,
        out_shape=tuple(VMEM(shape, dtype) for shape, dtype in outs),
        in_specs=specs,
        out_specs=tuple(pl.BlockSpec(memory_space=VMEM) for _ in outs),
        scratch_shapes=scratch,
        compiler_params=pltpu.CompilerParams(vmem_limit_bytes=limit),
        cost_estimate=pl.CostEstimate(flops=flops, transcendentals=0, bytes_accessed=0) if flops else None,
        name=name,
    )(*args)


def in_hbm(*arrays):
    return [pltpu.with_memory_space_constraint(a, pltpu.MemorySpace.HBM) for a in arrays]


def pack_kernel(tok_ref, ids_ref, gw_ref, out_ref, meta_ref):
    rows, width = tok_ref.shape
    out_ref[:, :width] = tok_ref[...]
    w = gw_ref[...]
    high = w.astype(BF16).astype(F32)
    mid = (w - high).astype(BF16).astype(F32)
    meta_ref[...] = jnp.zeros(meta_ref.shape, F32)
    meta_ref[0:2, 0:rows] = ids_ref[...].astype(F32)
    meta_ref[2:4, 0:rows] = high
    meta_ref[4:6, 0:rows] = mid
    meta_ref[6:8, 0:rows] = w - high - mid
    out_ref[:, width:] = meta_ref[...].astype(BF16)


def packed(tokens, ids, gate_weights):
    rows, width = tokens.shape
    return pl.pallas_call(
        pack_kernel,
        out_shape=VMEM((rows, width + META), BF16),
        out_specs=pl.BlockSpec(memory_space=VMEM),
        scratch_shapes=[pltpu.VMEM((8, META), F32)],
        compiler_params=pltpu.CompilerParams(vmem_limit_bytes=2**20),
        name="pack",
    )(*in_hbm(tokens, ids.T, gate_weights.T))


def placement(meta, zh, block):
    rows = 8
    meta = meta.astype(F32)
    r = iota((X * 2 * SLOTS, rows), 0)
    expert = ((r // (2 * SLOTS)) * ZH + zh).astype(F32)
    named = jnp.where((meta[0:1, :rows] == expert) | (meta[1:2, :rows] == expert), 1.0, 0.0)
    before = jnp.where(iota((rows, rows), 0) < iota((rows, rows), 1), 1.0, 0.0)
    rank = dot(named.astype(BF16), before.astype(BF16))
    mine = (r // SLOTS) % 2 == block
    return jnp.where(mine & (named > 0.5) & (rank == (r % SLOTS).astype(F32)), 1.0, 0.0).astype(BF16)


def place_kernel(zh_ref, own_ref, other_ref, out_ref, both_ref):
    width = out_ref.shape[-1]
    zh = zh_ref[0]
    both_ref[0:8] = own_ref[:, :width]
    both_ref[8:16] = other_ref[:, :width]
    places = [placement(own_ref[:, width:], zh, 0), placement(other_ref[:, width:], zh, 1)]
    slots = dot(jnp.concatenate(places, axis=1), both_ref[...]).astype(BF16)
    for x in range(X):
        for y in range(Y):
            out_ref[x * Y + y] = slots[x * 2 * SLOTS : (x + 1) * 2 * SLOTS]


def placed(zh, own, other):
    width = own.shape[1] - META
    outs = [((X * Y, 2 * SLOTS, width), BF16)]
    return call(place_kernel, outs, (zh, own, other), "place", [pltpu.VMEM((16, width), BF16)])[0]


BLOCK = 256


def hidden_units(rows, wg_ref, wu_ref, out_ref):
    for start in range(0, out_ref.shape[1], BLOCK):
        gate = dot(rows, wg_ref[0, :, start : start + BLOCK])
        up = dot(rows, wu_ref[0, :, start : start + BLOCK])
        out_ref[:, start : start + BLOCK] = (gate / (1.0 + jnp.exp(-gate)) * up).astype(BF16)


def down(hidden, wd_ref, out_ref):
    for start in range(0, out_ref.shape[1], BLOCK):
        out_ref[:, start : start + BLOCK] = dot(hidden, wd_ref[0, :, start : start + BLOCK]).astype(out_ref.dtype)


def hidden_kernel(rows_ref, wg_ref, wu_ref, out_ref):
    hidden_units(rows_ref[...], wg_ref, wu_ref, out_ref)


def down_kernel(hidden_ref, wd_ref, out_ref):
    down(hidden_ref[...], wd_ref, out_ref)


def expert_kernel(rows_ref, wg_ref, wu_ref, wd_ref, out_ref, hidden_ref):
    hidden_units(rows_ref[...], wg_ref, wu_ref, hidden_ref)
    down(hidden_ref[...], wd_ref, out_ref)


PIECES = 4


def load_kernel(*refs):
    sources, targets, sems = refs[1:4], refs[4:7], refs[7]
    copies = []
    for source, target in zip(sources, targets):
        rows = source.shape[1] // PIECES
        for piece in range(PIECES):
            part = pl.ds(piece * rows, rows)
            copies.append(pltpu.make_async_copy(source.at[0, part], target.at[0, part], sems.at[len(copies)]))
    for copy in copies:
        copy.start()
    for copy in copies:
        copy.wait()


def loaded(after, *weights):
    anywhere = pl.BlockSpec(memory_space=pl.ANY)
    return pl.pallas_call(
        load_kernel,
        out_shape=tuple(VMEM(w.shape, w.dtype) for w in weights),
        in_specs=[anywhere] * (1 + len(weights)),
        out_specs=tuple(pl.BlockSpec(memory_space=VMEM) for _ in weights),
        scratch_shapes=[pltpu.SemaphoreType.DMA((len(weights) * PIECES,))],
        cost_estimate=pl.CostEstimate(flops=0, transcendentals=0, bytes_accessed=2 * sum(w.size * 2 for w in weights)),
        compiler_params=pltpu.CompilerParams(vmem_limit_bytes=2**20),
        name="load",
    )(after, *in_hbm(*weights))


def mixing(meta, zh, block):
    rows = 8
    eye = jnp.where(iota((8, 8), 0) == iota((8, 8), 1), 1.0, 0.0).astype(BF16)
    fields = dot(eye, meta[:, :rows], ((1,), (1,)))
    lanes = X * Y * 2 * SLOTS
    r = iota((rows, lanes), 1)
    expert = ((r // (Y * 2 * SLOTS)) * ZH + zh).astype(F32)
    first = fields[:, 0:1] == expert
    second = fields[:, 1:2] == expert
    named = jnp.where(first | second, 1.0, 0.0)
    before = jnp.where(iota((rows, rows), 1) < iota((rows, rows), 0), 1.0, 0.0)
    rank = dot(before.astype(BF16), named.astype(BF16))
    w0 = fields[:, 2:3] + fields[:, 4:5] + fields[:, 6:7]
    w1 = fields[:, 3:4] + fields[:, 5:6] + fields[:, 7:8]
    mine = (r // SLOTS) % 2 == block
    weight = jnp.where(first, w0, jnp.where(second, w1, 0.0))
    return jnp.where(mine & (rank == (r % SLOTS).astype(F32)), weight, 0.0)


def split(weights):
    high = weights.astype(BF16).astype(F32)
    mid = (weights - high).astype(BF16).astype(F32)
    return jnp.concatenate([high, mid, weights - high - mid], axis=0).astype(BF16)


def weights_kernel(zh_ref, own_ref, other_ref, own_out, other_out):
    width = own_ref.shape[1] - META
    own_out[...] = split(mixing(own_ref[:, width:], zh_ref[0], 0))
    other_out[...] = split(mixing(other_ref[:, width:], zh_ref[0], 1))


def mix_kernel(weights_ref, rows_ref, out_ref):
    total = dot(weights_ref[...], rows_ref[...])
    out_ref[...] = (total[0:8] + total[8:16] + total[16:24]).astype(out_ref.dtype)


def mix(weights, rows, dtype, name):
    return call(mix_kernel, [((8, rows.shape[1]), dtype)], (weights, rows), name, flops=2 * weights.shape[0] * rows.size)[0]


def swapped(value, axis):
    return lax.ppermute(value, axis, [(0, 1), (1, 0)])


def on_device(tokens, expert_ids, gate_weights, gate_proj, up_proj, down_proj):
    width = tokens.shape[1]
    units = gate_proj.shape[2]
    zh = lax.axis_index("zh").astype(jnp.int32).reshape(1)
    own = packed(tokens, expert_ids, gate_weights)
    other = swapped(own, "zh")
    weights = loaded(own, gate_proj, up_proj, down_proj)
    other, (wg, wu, wd) = lax.optimization_barrier((other, weights))
    slots = placed(zh, own, other)
    half = slots.shape[0] * slots.shape[1]
    rows = lax.all_to_all(slots, ("x", "y"), 0, 0, tiled=True).reshape(half, width)
    core_rows = swapped(rows, "core")
    third = 2 * half * width * units
    hidden = call(hidden_kernel, [((half, units), BF16)], (rows, wg, wu), "hidden", flops=2 * third)[0]
    core_rows, hidden = lax.optimization_barrier((core_rows, hidden))
    scratch = [pltpu.VMEM((half, units), BF16)]
    core_part = call(expert_kernel, [((half, width), BF16)], (core_rows, wg, wu, wd), "expert", scratch, flops=3 * third)[0]
    core_part, own, other = lax.optimization_barrier((core_part, own, other))
    arrived = swapped(core_part, "core")
    part = call(down_kernel, [((half, width), F32)], (hidden, wd), "down", flops=third)[0]
    outs = [((24, half), BF16), ((24, half), BF16)]
    mixers = call(weights_kernel, outs, (zh, own, other), "weights", flops=2**28)
    arrived, part, (own_weights, other_weights) = lax.optimization_barrier((arrived, part, mixers))
    pair = (part + arrived.astype(F32)).astype(BF16).reshape(slots.shape)
    back = lax.all_to_all(pair, ("x", "y"), 0, 0, tiled=True)
    back = back.reshape(half, width)
    arriving = swapped(mix(other_weights, back, BF16, "mix_other"), "zh")
    keep = mix(own_weights, back, F32, "mix_own")
    return (keep + arriving.astype(F32)).astype(BF16)


def solution(mesh):
    dp = mesh.shape["dp"]
    fine = Mesh(mesh.devices.reshape(dp, X, ZH, Y, CORE), ("dp", "x", "zh", "y", "core"))
    every = P(("dp", "x", "zh", "y", "core"), None)
    return jax.shard_map(
        on_device,
        mesh=fine,
        in_specs=(
            every,
            every,
            every,
            P(("x", "zh"), None, ("y", "core")),
            P(("x", "zh"), None, ("y", "core")),
            P(("x", "zh"), ("y", "core"), None),
        ),
        out_specs=every,
        check_vma=False,
    )
```

```python
import functools

import jax
import jax.numpy as jnp
from jax import lax
from jax.experimental import pallas as pl
from jax.experimental.pallas import tpu as pltpu
from jax.sharding import Mesh, PartitionSpec as P

X, ZH, Y, CORE = 4, 2, 4, 2
SLOTS = 4
META = 128
BF16, F32 = jnp.bfloat16, jnp.float32
VMEM = pltpu.MemorySpace.VMEM
SMEM = pltpu.MemorySpace.SMEM


def dot(a, b, contract=((1,), (0,))):
    return lax.dot_general(a, b, (contract, ((), ())), preferred_element_type=F32)


def iota(shape, dim):
    return lax.broadcasted_iota(jnp.int32, shape, dim)


def call(kernel, outs, args, name, scratch=(), limit=8 * 2**20, flops=0):
    specs = [pl.BlockSpec(memory_space=SMEM if a.size == 1 else VMEM) for a in args]
    args = [a if a.size == 1 else pltpu.with_memory_space_constraint(a, VMEM) for a in args]
    return pl.pallas_call(
        kernel,
        out_shape=tuple(VMEM(shape, dtype) for shape, dtype in outs),
        in_specs=specs,
        out_specs=tuple(pl.BlockSpec(memory_space=VMEM) for _ in outs),
        scratch_shapes=scratch,
        compiler_params=pltpu.CompilerParams(vmem_limit_bytes=limit),
        cost_estimate=pl.CostEstimate(flops=flops, transcendentals=0, bytes_accessed=0) if flops else None,
        name=name,
    )(*args)


def in_hbm(*arrays):
    return [pltpu.with_memory_space_constraint(a, pltpu.MemorySpace.HBM) for a in arrays]


def pack_kernel(tok_ref, ids_ref, gw_ref, out_ref, meta_ref):
    rows, width = tok_ref.shape
    out_ref[:, :width] = tok_ref[...]
    w = gw_ref[...]
    high = w.astype(BF16).astype(F32)
    mid = (w - high).astype(BF16).astype(F32)
    meta_ref[...] = jnp.zeros(meta_ref.shape, F32)
    meta_ref[0:2, 0:rows] = ids_ref[...].astype(F32)
    meta_ref[2:4, 0:rows] = high
    meta_ref[4:6, 0:rows] = mid
    meta_ref[6:8, 0:rows] = w - high - mid
    out_ref[:, width:] = meta_ref[...].astype(BF16)


def packed(tokens, ids, gate_weights):
    rows, width = tokens.shape
    return pl.pallas_call(
        pack_kernel,
        out_shape=VMEM((rows, width + META), BF16),
        out_specs=pl.BlockSpec(memory_space=VMEM),
        scratch_shapes=[pltpu.VMEM((8, META), F32)],
        compiler_params=pltpu.CompilerParams(vmem_limit_bytes=2**20),
        name="pack",
    )(*in_hbm(tokens, ids.T, gate_weights.T))


def placement(meta, zh, block):
    rows = 8
    meta = meta.astype(F32)
    r = iota((X * 2 * SLOTS, rows), 0)
    expert = ((r // (2 * SLOTS)) * ZH + zh).astype(F32)
    named = jnp.where((meta[0:1, :rows] == expert) | (meta[1:2, :rows] == expert), 1.0, 0.0)
    before = jnp.where(iota((rows, rows), 0) < iota((rows, rows), 1), 1.0, 0.0)
    rank = dot(named.astype(BF16), before.astype(BF16))
    mine = (r // SLOTS) % 2 == block
    return jnp.where(mine & (named > 0.5) & (rank == (r % SLOTS).astype(F32)), 1.0, 0.0).astype(BF16)


def place_kernel(zh_ref, own_ref, other_ref, out_ref, both_ref):
    width = out_ref.shape[-1]
    zh = zh_ref[0]
    both_ref[0:8] = own_ref[:, :width]
    both_ref[8:16] = other_ref[:, :width]
    places = [placement(own_ref[:, width:], zh, 0), placement(other_ref[:, width:], zh, 1)]
    slots = dot(jnp.concatenate(places, axis=1), both_ref[...]).astype(BF16)
    for x in range(X):
        for y in range(Y):
            out_ref[x * Y + y] = slots[x * 2 * SLOTS : (x + 1) * 2 * SLOTS]


def placed(zh, own, other):
    width = own.shape[1] - META
    outs = [((X * Y, 2 * SLOTS, width), BF16)]
    return call(place_kernel, outs, (zh, own, other), "place", [pltpu.VMEM((16, width), BF16)])[0]


BLOCK = 256


def hidden_units(rows, wg_ref, wu_ref, out_ref):
    for start in range(0, out_ref.shape[1], BLOCK):
        gate = dot(rows, wg_ref[0, :, start : start + BLOCK])
        up = dot(rows, wu_ref[0, :, start : start + BLOCK])
        out_ref[:, start : start + BLOCK] = (gate / (1.0 + jnp.exp(-gate)) * up).astype(BF16)


def down(hidden, wd_ref, out_ref):
    for start in range(0, out_ref.shape[1], BLOCK):
        out_ref[:, start : start + BLOCK] = dot(hidden, wd_ref[0, :, start : start + BLOCK]).astype(out_ref.dtype)


def hidden_kernel(rows_ref, wg_ref, wu_ref, out_ref):
    hidden_units(rows_ref[...], wg_ref, wu_ref, out_ref)


def down_kernel(hidden_ref, wd_ref, out_ref):
    down(hidden_ref[...], wd_ref, out_ref)


def expert_kernel(rows_ref, wg_ref, wu_ref, wd_ref, out_ref, hidden_ref):
    hidden_units(rows_ref[...], wg_ref, wu_ref, hidden_ref)
    down(hidden_ref[...], wd_ref, out_ref)


PIECES = 4


def load_kernel(*refs):
    sources, targets, sems = refs[1:4], refs[4:7], refs[7]
    copies = []
    for source, target in zip(sources, targets):
        rows = source.shape[1] // PIECES
        for piece in range(PIECES):
            part = pl.ds(piece * rows, rows)
            copies.append(pltpu.make_async_copy(source.at[0, part], target.at[0, part], sems.at[len(copies)]))
    for copy in copies:
        copy.start()
    for copy in copies:
        copy.wait()


def loaded(after, *weights):
    anywhere = pl.BlockSpec(memory_space=pl.ANY)
    return pl.pallas_call(
        load_kernel,
        out_shape=tuple(VMEM(w.shape, w.dtype) for w in weights),
        in_specs=[anywhere] * (1 + len(weights)),
        out_specs=tuple(pl.BlockSpec(memory_space=VMEM) for _ in weights),
        scratch_shapes=[pltpu.SemaphoreType.DMA((len(weights) * PIECES,))],
        cost_estimate=pl.CostEstimate(flops=0, transcendentals=0, bytes_accessed=2 * sum(w.size * 2 for w in weights)),
        compiler_params=pltpu.CompilerParams(vmem_limit_bytes=2**20),
        name="load",
    )(after, *in_hbm(*weights))


def mixing(meta, zh, block):
    rows = 8
    eye = jnp.where(iota((8, 8), 0) == iota((8, 8), 1), 1.0, 0.0).astype(BF16)
    fields = dot(eye, meta[:, :rows], ((1,), (1,)))
    lanes = X * Y * 2 * SLOTS
    r = iota((rows, lanes), 1)
    expert = ((r // (Y * 2 * SLOTS)) * ZH + zh).astype(F32)
    first = fields[:, 0:1] == expert
    second = fields[:, 1:2] == expert
    named = jnp.where(first | second, 1.0, 0.0)
    before = jnp.where(iota((rows, rows), 1) < iota((rows, rows), 0), 1.0, 0.0)
    rank = dot(before.astype(BF16), named.astype(BF16))
    w0 = fields[:, 2:3] + fields[:, 4:5] + fields[:, 6:7]
    w1 = fields[:, 3:4] + fields[:, 5:6] + fields[:, 7:8]
    mine = (r // SLOTS) % 2 == block
    weight = jnp.where(first, w0, jnp.where(second, w1, 0.0))
    return jnp.where(mine & (rank == (r % SLOTS).astype(F32)), weight, 0.0)


def split(weights):
    high = weights.astype(BF16).astype(F32)
    mid = (weights - high).astype(BF16).astype(F32)
    return jnp.concatenate([high, mid, weights - high - mid], axis=0).astype(BF16)


def weights_kernel(zh_ref, own_ref, other_ref, own_out, other_out):
    width = own_ref.shape[1] - META
    own_out[...] = split(mixing(own_ref[:, width:], zh_ref[0], 0))
    other_out[...] = split(mixing(other_ref[:, width:], zh_ref[0], 1))


def mix_kernel(weights_ref, rows_ref, out_ref):
    total = dot(weights_ref[...], rows_ref[...])
    out_ref[...] = (total[0:8] + total[8:16] + total[16:24]).astype(out_ref.dtype)


def mix(weights, rows, dtype, name):
    return call(mix_kernel, [((8, rows.shape[1]), dtype)], (weights, rows), name, flops=2 * weights.shape[0] * rows.size)[0]


def both_kernel(own_ref, other_ref, rows_ref, keep_ref, send_ref):
    total = dot(jnp.concatenate([own_ref[...], other_ref[...]], axis=0), rows_ref[...])
    keep_ref[...] = total[0:8] + total[8:16] + total[16:24]
    send_ref[...] = (total[24:32] + total[32:40] + total[40:48]).astype(BF16)


def final_kernel(zh_ref, keep_ref, gathered_ref, out_ref):
    out_ref[...] = (keep_ref[...] + gathered_ref[1 - zh_ref[0]].astype(F32)).astype(BF16)


def swapped(value, axis):
    return lax.ppermute(value, axis, [(0, 1), (1, 0)])


def on_device(tokens, expert_ids, gate_weights, gate_proj, up_proj, down_proj):
    width = tokens.shape[1]
    units = gate_proj.shape[2]
    zh = lax.axis_index("zh").astype(jnp.int32).reshape(1)
    own = packed(tokens, expert_ids, gate_weights)
    other = swapped(own, "zh")
    weights = loaded(own, gate_proj, up_proj, down_proj)
    other, (wg, wu, wd) = lax.optimization_barrier((other, weights))
    slots = placed(zh, own, other)
    half = slots.shape[0] * slots.shape[1]
    rows = lax.all_to_all(slots, ("x", "y"), 0, 0, tiled=True).reshape(half, width)
    core_rows = swapped(rows, "core")
    third = 2 * half * width * units
    hidden = call(hidden_kernel, [((half, units), BF16)], (rows, wg, wu), "hidden", flops=2 * third)[0]
    core_rows, hidden = lax.optimization_barrier((core_rows, hidden))
    scratch = [pltpu.VMEM((half, units), BF16)]
    core_part = call(expert_kernel, [((half, width), BF16)], (core_rows, wg, wu, wd), "expert", scratch, flops=3 * third)[0]
    core_part, own, other = lax.optimization_barrier((core_part, own, other))
    arrived = swapped(core_part, "core")
    part = call(down_kernel, [((half, width), F32)], (hidden, wd), "down", flops=third)[0]
    outs = [((24, half), BF16), ((24, half), BF16)]
    mixers = call(weights_kernel, outs, (zh, own, other), "weights", flops=2**28)
    arrived, part, (own_weights, other_weights) = lax.optimization_barrier((arrived, part, mixers))
    pair = (part + arrived.astype(F32)).astype(BF16).reshape(slots.shape)
    back = lax.all_to_all(pair, ("x", "y"), 0, 0, tiled=True)
    outs = [((8, width), F32), ((8, width), BF16)]
    keep, send = call(both_kernel, outs, (own_weights, other_weights, back.reshape(half, width)), "mix")
    gathered = lax.all_gather(send, "zh")
    return pl.pallas_call(
        final_kernel,
        out_shape=jax.ShapeDtypeStruct((8, width), BF16),
        in_specs=[pl.BlockSpec(memory_space=SMEM), pl.BlockSpec(memory_space=VMEM), pl.BlockSpec(memory_space=VMEM)],
        out_specs=pl.BlockSpec(memory_space=VMEM),
        compiler_params=pltpu.CompilerParams(vmem_limit_bytes=2**20),
        name="final",
    )(zh, pltpu.with_memory_space_constraint(keep, VMEM), pltpu.with_memory_space_constraint(gathered, VMEM))


def solution(mesh):
    dp = mesh.shape["dp"]
    fine = Mesh(mesh.devices.reshape(dp, X, ZH, Y, CORE), ("dp", "x", "zh", "y", "core"))
    every = P(("dp", "x", "zh", "y", "core"), None)
    return jax.shard_map(
        on_device,
        mesh=fine,
        in_specs=(
            every,
            every,
            every,
            P(("x", "zh"), None, ("y", "core")),
            P(("x", "zh"), None, ("y", "core")),
            P(("x", "zh"), ("y", "core"), None),
        ),
        out_specs=every,
        check_vma=False,
    )
```

```python
import functools

import jax
import jax.numpy as jnp
from jax import lax
from jax.experimental import pallas as pl
from jax.experimental.pallas import tpu as pltpu
from jax.sharding import Mesh, PartitionSpec as P

X, ZH, Y, CORE = 4, 2, 4, 2
SLOTS = 4
META = 128
BF16, F32 = jnp.bfloat16, jnp.float32
VMEM = pltpu.MemorySpace.VMEM
SMEM = pltpu.MemorySpace.SMEM


def dot(a, b, contract=((1,), (0,))):
    return lax.dot_general(a, b, (contract, ((), ())), preferred_element_type=F32)


def iota(shape, dim):
    return lax.broadcasted_iota(jnp.int32, shape, dim)


def call(kernel, outs, args, name, scratch=(), limit=8 * 2**20, flops=0):
    specs = [pl.BlockSpec(memory_space=SMEM if a.size == 1 else VMEM) for a in args]
    args = [a if a.size == 1 else pltpu.with_memory_space_constraint(a, VMEM) for a in args]
    return pl.pallas_call(
        kernel,
        out_shape=tuple(VMEM(shape, dtype) for shape, dtype in outs),
        in_specs=specs,
        out_specs=tuple(pl.BlockSpec(memory_space=VMEM) for _ in outs),
        scratch_shapes=scratch,
        compiler_params=pltpu.CompilerParams(vmem_limit_bytes=limit),
        cost_estimate=pl.CostEstimate(flops=flops, transcendentals=0, bytes_accessed=0) if flops else None,
        name=name,
    )(*args)


def in_hbm(*arrays):
    return [pltpu.with_memory_space_constraint(a, pltpu.MemorySpace.HBM) for a in arrays]


def pack_kernel(tok_ref, ids_ref, gw_ref, out_ref, meta_ref):
    rows, width = tok_ref.shape
    out_ref[:, :width] = tok_ref[...]
    w = gw_ref[...]
    high = w.astype(BF16).astype(F32)
    mid = (w - high).astype(BF16).astype(F32)
    meta_ref[...] = jnp.zeros(meta_ref.shape, F32)
    meta_ref[0:2, 0:rows] = ids_ref[...].astype(F32)
    meta_ref[2:4, 0:rows] = high
    meta_ref[4:6, 0:rows] = mid
    meta_ref[6:8, 0:rows] = w - high - mid
    out_ref[:, width:] = meta_ref[...].astype(BF16)


def packed(tokens, ids, gate_weights):
    rows, width = tokens.shape
    return pl.pallas_call(
        pack_kernel,
        out_shape=VMEM((rows, width + META), BF16),
        out_specs=pl.BlockSpec(memory_space=VMEM),
        scratch_shapes=[pltpu.VMEM((8, META), F32)],
        compiler_params=pltpu.CompilerParams(vmem_limit_bytes=2**20),
        name="pack",
    )(*in_hbm(tokens, ids.T, gate_weights.T))


def placement(meta, zh, block):
    rows = 8
    meta = meta.astype(F32)
    r = iota((X * 2 * SLOTS, rows), 0)
    expert = ((r // (2 * SLOTS)) * ZH + zh).astype(F32)
    named = jnp.where((meta[0:1, :rows] == expert) | (meta[1:2, :rows] == expert), 1.0, 0.0)
    before = jnp.where(iota((rows, rows), 0) < iota((rows, rows), 1), 1.0, 0.0)
    rank = dot(named.astype(BF16), before.astype(BF16))
    mine = (r // SLOTS) % 2 == block
    return jnp.where(mine & (named > 0.5) & (rank == (r % SLOTS).astype(F32)), 1.0, 0.0).astype(BF16)


def place_kernel(zh_ref, own_ref, halves_ref, out_ref, both_ref):
    width = out_ref.shape[-1]
    zh = zh_ref[0]
    both_ref[0:8] = own_ref[:, :width]
    both_ref[8:16] = halves_ref[1 - zh, :, :width]
    places = [placement(own_ref[:, width:], zh, 0), placement(halves_ref[1 - zh, :, width:], zh, 1)]
    slots = dot(jnp.concatenate(places, axis=1), both_ref[...]).astype(BF16)
    for x in range(X):
        for y in range(Y):
            out_ref[x * Y + y] = slots[x * 2 * SLOTS : (x + 1) * 2 * SLOTS]


def placed(zh, own, halves):
    width = own.shape[1] - META
    outs = [((X * Y, 2 * SLOTS, width), BF16)]
    return call(place_kernel, outs, (zh, own, halves), "place", [pltpu.VMEM((16, width), BF16)], flops=2**35)[0]


BLOCK = 256


def hidden_units(rows, wg_ref, wu_ref, out_ref):
    for start in range(0, out_ref.shape[1], BLOCK):
        gate = dot(rows, wg_ref[0, :, start : start + BLOCK])
        up = dot(rows, wu_ref[0, :, start : start + BLOCK])
        out_ref[:, start : start + BLOCK] = (gate / (1.0 + jnp.exp(-gate)) * up).astype(BF16)


def down(hidden, wd_ref, out_ref):
    for start in range(0, out_ref.shape[1], BLOCK):
        out_ref[:, start : start + BLOCK] = dot(hidden, wd_ref[0, :, start : start + BLOCK]).astype(out_ref.dtype)


def hidden_kernel(rows_ref, wg_ref, wu_ref, out_ref):
    hidden_units(rows_ref[...], wg_ref, wu_ref, out_ref)


def down_kernel(hidden_ref, wd_ref, out_ref):
    down(hidden_ref[...], wd_ref, out_ref)


def expert_kernel(rows_ref, wg_ref, wu_ref, wd_ref, out_ref, hidden_ref):
    hidden_units(rows_ref[...], wg_ref, wu_ref, hidden_ref)
    down(hidden_ref[...], wd_ref, out_ref)


def mixing(meta, zh, block):
    rows = 8
    eye = jnp.where(iota((8, 8), 0) == iota((8, 8), 1), 1.0, 0.0).astype(BF16)
    fields = dot(eye, meta[:, :rows], ((1,), (1,)))
    lanes = X * Y * 2 * SLOTS
    r = iota((rows, lanes), 1)
    expert = ((r // (Y * 2 * SLOTS)) * ZH + zh).astype(F32)
    first = fields[:, 0:1] == expert
    second = fields[:, 1:2] == expert
    named = jnp.where(first | second, 1.0, 0.0)
    before = jnp.where(iota((rows, rows), 1) < iota((rows, rows), 0), 1.0, 0.0)
    rank = dot(before.astype(BF16), named.astype(BF16))
    w0 = fields[:, 2:3] + fields[:, 4:5] + fields[:, 6:7]
    w1 = fields[:, 3:4] + fields[:, 5:6] + fields[:, 7:8]
    mine = (r // SLOTS) % 2 == block
    weight = jnp.where(first, w0, jnp.where(second, w1, 0.0))
    return jnp.where(mine & (rank == (r % SLOTS).astype(F32)), weight, 0.0)


def split(weights):
    high = weights.astype(BF16).astype(F32)
    mid = (weights - high).astype(BF16).astype(F32)
    return jnp.concatenate([high, mid, weights - high - mid], axis=0).astype(BF16)


def weights_kernel(zh_ref, own_ref, halves_ref, own_out, other_out):
    width = own_ref.shape[1] - META
    own_out[...] = split(mixing(own_ref[:, width:], zh_ref[0], 0))
    other_out[...] = split(mixing(halves_ref[1 - zh_ref[0], :, width:], zh_ref[0], 1))


def mix_kernel(weights_ref, rows_ref, out_ref):
    total = dot(weights_ref[...], rows_ref[...])
    out_ref[...] = (total[0:8] + total[8:16] + total[16:24]).astype(out_ref.dtype)


def mix(weights, rows, dtype, name):
    return call(mix_kernel, [((8, rows.shape[1]), dtype)], (weights, rows), name, flops=2 * weights.shape[0] * rows.size)[0]


def both_kernel(own_ref, other_ref, rows_ref, keep_ref, send_ref):
    total = dot(jnp.concatenate([own_ref[...], other_ref[...]], axis=0), rows_ref[...])
    keep_ref[...] = total[0:8] + total[8:16] + total[16:24]
    send_ref[...] = (total[24:32] + total[32:40] + total[40:48]).astype(BF16)


def final_kernel(zh_ref, keep_ref, gathered_ref, out_ref):
    out_ref[...] = (keep_ref[...] + gathered_ref[1 - zh_ref[0]].astype(F32)).astype(BF16)


def swapped(value, axis):
    return lax.ppermute(value, axis, [(0, 1), (1, 0)])


def on_device(tokens, expert_ids, gate_weights, gate_proj, up_proj, down_proj):
    width = tokens.shape[1]
    units = gate_proj.shape[2]
    zh = lax.axis_index("zh").astype(jnp.int32).reshape(1)
    own = packed(tokens, expert_ids, gate_weights)
    halves = lax.all_gather(own, "zh")
    wg, wu, wd = gate_proj, up_proj, down_proj
    slots = placed(zh, own, halves)
    half = slots.shape[0] * slots.shape[1]
    rows = lax.all_to_all(slots, ("x", "y"), 0, 0, tiled=True).reshape(half, width)
    core_rows = swapped(rows, "core")
    third = 2 * half * width * units
    hidden = call(hidden_kernel, [((half, units), BF16)], (rows, wg, wu), "hidden", flops=2 * third)[0]
    core_rows, hidden = lax.optimization_barrier((core_rows, hidden))
    scratch = [pltpu.VMEM((half, units), BF16)]
    core_part = call(expert_kernel, [((half, width), BF16)], (core_rows, wg, wu, wd), "expert", scratch, flops=3 * third)[0]
    core_part, own, halves = lax.optimization_barrier((core_part, own, halves))
    arrived = swapped(core_part, "core")
    part = call(down_kernel, [((half, width), F32)], (hidden, wd), "down", flops=third)[0]
    outs = [((24, half), BF16), ((24, half), BF16)]
    mixers = call(weights_kernel, outs, (zh, own, halves), "weights", flops=2**28)
    arrived, part, (own_weights, other_weights) = lax.optimization_barrier((arrived, part, mixers))
    pair = (part + arrived.astype(F32)).astype(BF16).reshape(slots.shape)
    back = lax.all_to_all(pair, ("x", "y"), 0, 0, tiled=True)
    outs = [((8, width), F32), ((8, width), BF16)]
    keep, send = call(both_kernel, outs, (own_weights, other_weights, back.reshape(half, width)), "mix")
    gathered = lax.all_gather(send, "zh")
    return pl.pallas_call(
        final_kernel,
        out_shape=jax.ShapeDtypeStruct((8, width), BF16),
        in_specs=[pl.BlockSpec(memory_space=SMEM), pl.BlockSpec(memory_space=VMEM), pl.BlockSpec(memory_space=VMEM)],
        out_specs=pl.BlockSpec(memory_space=VMEM),
        compiler_params=pltpu.CompilerParams(vmem_limit_bytes=2**20),
        name="final",
    )(zh, pltpu.with_memory_space_constraint(keep, VMEM), pltpu.with_memory_space_constraint(gathered, VMEM))


def solution(mesh):
    dp = mesh.shape["dp"]
    fine = Mesh(mesh.devices.reshape(dp, X, ZH, Y, CORE), ("dp", "x", "zh", "y", "core"))
    every = P(("dp", "x", "zh", "y", "core"), None)
    return jax.shard_map(
        on_device,
        mesh=fine,
        in_specs=(
            every,
            every,
            every,
            P(("x", "zh"), None, ("y", "core")),
            P(("x", "zh"), None, ("y", "core")),
            P(("x", "zh"), ("y", "core"), None),
        ),
        out_specs=every,
        check_vma=False,
    )
```

```python
import functools

import jax
import jax.numpy as jnp
from jax import lax
from jax.experimental import pallas as pl
from jax.experimental.pallas import tpu as pltpu
from jax.sharding import Mesh, PartitionSpec as P

X, ZH, Y, CORE = 4, 2, 4, 2
SLOTS = 4
META = 128
BF16, F32 = jnp.bfloat16, jnp.float32
VMEM = pltpu.MemorySpace.VMEM
SMEM = pltpu.MemorySpace.SMEM


def dot(a, b, contract=((1,), (0,))):
    return lax.dot_general(a, b, (contract, ((), ())), preferred_element_type=F32)


def iota(shape, dim):
    return lax.broadcasted_iota(jnp.int32, shape, dim)


def call(kernel, outs, args, name, scratch=(), limit=8 * 2**20, flops=0):
    specs = [pl.BlockSpec(memory_space=SMEM if a.size == 1 else VMEM) for a in args]
    args = [a if a.size == 1 else pltpu.with_memory_space_constraint(a, VMEM) for a in args]
    return pl.pallas_call(
        kernel,
        out_shape=tuple(VMEM(shape, dtype) for shape, dtype in outs),
        in_specs=specs,
        out_specs=tuple(pl.BlockSpec(memory_space=VMEM) for _ in outs),
        scratch_shapes=scratch,
        compiler_params=pltpu.CompilerParams(vmem_limit_bytes=limit),
        cost_estimate=pl.CostEstimate(flops=flops, transcendentals=0, bytes_accessed=0) if flops else None,
        name=name,
    )(*args)


def in_hbm(*arrays):
    return [pltpu.with_memory_space_constraint(a, pltpu.MemorySpace.HBM) for a in arrays]


def pack_kernel(tok_ref, ids_ref, gw_ref, out_ref, meta_ref):
    rows, width = tok_ref.shape
    out_ref[:, :width] = tok_ref[...]
    w = gw_ref[...]
    high = w.astype(BF16).astype(F32)
    mid = (w - high).astype(BF16).astype(F32)
    meta_ref[...] = jnp.zeros(meta_ref.shape, F32)
    meta_ref[0:2, 0:rows] = ids_ref[...].astype(F32)
    meta_ref[2:4, 0:rows] = high
    meta_ref[4:6, 0:rows] = mid
    meta_ref[6:8, 0:rows] = w - high - mid
    out_ref[:, width:] = meta_ref[...].astype(BF16)


def packed(tokens, ids, gate_weights):
    rows, width = tokens.shape
    return pl.pallas_call(
        pack_kernel,
        out_shape=VMEM((rows, width + META), BF16),
        out_specs=pl.BlockSpec(memory_space=VMEM),
        scratch_shapes=[pltpu.VMEM((8, META), F32)],
        compiler_params=pltpu.CompilerParams(vmem_limit_bytes=2**20),
        name="pack",
    )(*in_hbm(tokens, ids.T, gate_weights.T))


def placement(meta, zh, block):
    rows = 8
    meta = meta.astype(F32)
    r = iota((X * 2 * SLOTS, rows), 0)
    expert = ((r // (2 * SLOTS)) * ZH + zh).astype(F32)
    named = jnp.where((meta[0:1, :rows] == expert) | (meta[1:2, :rows] == expert), 1.0, 0.0)
    before = jnp.where(iota((rows, rows), 0) < iota((rows, rows), 1), 1.0, 0.0)
    rank = dot(named.astype(BF16), before.astype(BF16))
    mine = (r // SLOTS) % 2 == block
    return jnp.where(mine & (named > 0.5) & (rank == (r % SLOTS).astype(F32)), 1.0, 0.0).astype(BF16)


def place_kernel(zh_ref, own_ref, halves_ref, out_ref, both_ref):
    width = out_ref.shape[-1]
    zh = zh_ref[0]
    both_ref[0:8] = own_ref[:, :width]
    both_ref[8:16] = halves_ref[1 - zh, :, :width]
    places = [placement(own_ref[:, width:], zh, 0), placement(halves_ref[1 - zh, :, width:], zh, 1)]
    slots = dot(jnp.concatenate(places, axis=1), both_ref[...]).astype(BF16)
    for x in range(X):
        for y in range(Y):
            out_ref[x * Y + y] = slots[x * 2 * SLOTS : (x + 1) * 2 * SLOTS]


def placed(zh, own, halves):
    width = own.shape[1] - META
    outs = [((X * Y, 2 * SLOTS, width), BF16)]
    return call(place_kernel, outs, (zh, own, halves), "place", [pltpu.VMEM((16, width), BF16)], flops=2**35)[0]


BLOCK = 512


def hidden_units(rows, wg_ref, wu_ref, out_ref):
    for start in range(0, out_ref.shape[1], BLOCK):
        gate = dot(rows, wg_ref[0, :, start : start + BLOCK])
        up = dot(rows, wu_ref[0, :, start : start + BLOCK])
        out_ref[:, start : start + BLOCK] = (gate / (1.0 + jnp.exp(-gate)) * up).astype(BF16)


def down(hidden, wd_ref, out_ref):
    for start in range(0, out_ref.shape[1], BLOCK):
        out_ref[:, start : start + BLOCK] = dot(hidden, wd_ref[0, :, start : start + BLOCK]).astype(out_ref.dtype)


def hidden_kernel(rows_ref, wg_ref, wu_ref, out_ref):
    hidden_units(rows_ref[...], wg_ref, wu_ref, out_ref)


def down_kernel(hidden_ref, wd_ref, out_ref):
    down(hidden_ref[...], wd_ref, out_ref)


def expert_kernel(rows_ref, wg_ref, wu_ref, wd_ref, out_ref, hidden_ref):
    hidden_units(rows_ref[...], wg_ref, wu_ref, hidden_ref)
    down(hidden_ref[...], wd_ref, out_ref)


def mixing(meta, zh, block):
    rows = 8
    eye = jnp.where(iota((8, 8), 0) == iota((8, 8), 1), 1.0, 0.0).astype(BF16)
    fields = dot(eye, meta[:, :rows], ((1,), (1,)))
    lanes = X * Y * 2 * SLOTS
    r = iota((rows, lanes), 1)
    expert = ((r // (Y * 2 * SLOTS)) * ZH + zh).astype(F32)
    first = fields[:, 0:1] == expert
    second = fields[:, 1:2] == expert
    named = jnp.where(first | second, 1.0, 0.0)
    before = jnp.where(iota((rows, rows), 1) < iota((rows, rows), 0), 1.0, 0.0)
    rank = dot(before.astype(BF16), named.astype(BF16))
    w0 = fields[:, 2:3] + fields[:, 4:5] + fields[:, 6:7]
    w1 = fields[:, 3:4] + fields[:, 5:6] + fields[:, 7:8]
    mine = (r // SLOTS) % 2 == block
    weight = jnp.where(first, w0, jnp.where(second, w1, 0.0))
    return jnp.where(mine & (rank == (r % SLOTS).astype(F32)), weight, 0.0)


def split(weights):
    high = weights.astype(BF16).astype(F32)
    mid = (weights - high).astype(BF16).astype(F32)
    return jnp.concatenate([high, mid, weights - high - mid], axis=0).astype(BF16)


def weights_kernel(zh_ref, own_ref, halves_ref, own_out, other_out):
    width = own_ref.shape[1] - META
    own_out[...] = split(mixing(own_ref[:, width:], zh_ref[0], 0))
    other_out[...] = split(mixing(halves_ref[1 - zh_ref[0], :, width:], zh_ref[0], 1))


def mix_kernel(weights_ref, rows_ref, out_ref):
    total = dot(weights_ref[...], rows_ref[...])
    out_ref[...] = (total[0:8] + total[8:16] + total[16:24]).astype(out_ref.dtype)


def mix(weights, rows, dtype, name):
    return call(mix_kernel, [((8, rows.shape[1]), dtype)], (weights, rows), name, flops=2 * weights.shape[0] * rows.size)[0]


def both_kernel(own_ref, other_ref, rows_ref, keep_ref, send_ref):
    total = dot(jnp.concatenate([own_ref[...], other_ref[...]], axis=0), rows_ref[...])
    keep_ref[...] = total[0:8] + total[8:16] + total[16:24]
    send_ref[...] = (total[24:32] + total[32:40] + total[40:48]).astype(BF16)


def final_kernel(zh_ref, keep_ref, gathered_ref, out_ref):
    out_ref[...] = (keep_ref[...] + gathered_ref[1 - zh_ref[0]].astype(F32)).astype(BF16)


def swapped(value, axis):
    return lax.ppermute(value, axis, [(0, 1), (1, 0)])


def on_device(tokens, expert_ids, gate_weights, gate_proj, up_proj, down_proj):
    width = tokens.shape[1]
    units = gate_proj.shape[2]
    zh = lax.axis_index("zh").astype(jnp.int32).reshape(1)
    own = packed(tokens, expert_ids, gate_weights)
    halves = lax.all_gather(own, "zh")
    wg, wu, wd = gate_proj, up_proj, down_proj
    slots = placed(zh, own, halves)
    half = slots.shape[0] * slots.shape[1]
    rows = lax.all_to_all(slots, ("x", "y"), 0, 0, tiled=True).reshape(half, width)
    core_rows = swapped(rows, "core")
    third = 2 * half * width * units
    hidden = call(hidden_kernel, [((half, units), BF16)], (rows, wg, wu), "hidden", flops=2 * third)[0]
    core_rows, hidden = lax.optimization_barrier((core_rows, hidden))
    scratch = [pltpu.VMEM((half, units), BF16)]
    core_part = call(expert_kernel, [((half, width), BF16)], (core_rows, wg, wu, wd), "expert", scratch, flops=3 * third)[0]
    core_part, own, halves = lax.optimization_barrier((core_part, own, halves))
    arrived = swapped(core_part, "core")
    part = call(down_kernel, [((half, width), F32)], (hidden, wd), "down", flops=third)[0]
    outs = [((24, half), BF16), ((24, half), BF16)]
    mixers = call(weights_kernel, outs, (zh, own, halves), "weights", flops=2**28)
    arrived, part, (own_weights, other_weights) = lax.optimization_barrier((arrived, part, mixers))
    pair = (part + arrived.astype(F32)).astype(BF16).reshape(slots.shape)
    back = lax.all_to_all(pair, ("x", "y"), 0, 0, tiled=True)
    outs = [((8, width), F32), ((8, width), BF16)]
    keep, send = call(both_kernel, outs, (own_weights, other_weights, back.reshape(half, width)), "mix")
    gathered = lax.all_gather(send, "zh")
    return pl.pallas_call(
        final_kernel,
        out_shape=jax.ShapeDtypeStruct((8, width), BF16),
        in_specs=[pl.BlockSpec(memory_space=SMEM), pl.BlockSpec(memory_space=VMEM), pl.BlockSpec(memory_space=VMEM)],
        out_specs=pl.BlockSpec(memory_space=VMEM),
        compiler_params=pltpu.CompilerParams(vmem_limit_bytes=2**20),
        name="final",
    )(zh, pltpu.with_memory_space_constraint(keep, VMEM), pltpu.with_memory_space_constraint(gathered, VMEM))


def solution(mesh):
    dp = mesh.shape["dp"]
    fine = Mesh(mesh.devices.reshape(dp, X, ZH, Y, CORE), ("dp", "x", "zh", "y", "core"))
    every = P(("dp", "x", "zh", "y", "core"), None)
    return jax.shard_map(
        on_device,
        mesh=fine,
        in_specs=(
            every,
            every,
            every,
            P(("x", "zh"), None, ("y", "core")),
            P(("x", "zh"), None, ("y", "core")),
            P(("x", "zh"), ("y", "core"), None),
        ),
        out_specs=every,
        check_vma=False,
    )
```

```python
import functools

import jax
import jax.numpy as jnp
from jax import lax
from jax.experimental import pallas as pl
from jax.experimental.pallas import tpu as pltpu
from jax.sharding import Mesh, PartitionSpec as P

X, ZH, Y, CORE = 4, 2, 4, 2
SLOTS = 4
META = 128
BF16, F32 = jnp.bfloat16, jnp.float32
VMEM = pltpu.MemorySpace.VMEM
SMEM = pltpu.MemorySpace.SMEM


def dot(a, b, contract=((1,), (0,))):
    return lax.dot_general(a, b, (contract, ((), ())), preferred_element_type=F32)


def iota(shape, dim):
    return lax.broadcasted_iota(jnp.int32, shape, dim)


def call(kernel, outs, args, name, scratch=(), limit=8 * 2**20, flops=0):
    specs = [pl.BlockSpec(memory_space=SMEM if a.size == 1 else VMEM) for a in args]
    args = [a if a.size == 1 else pltpu.with_memory_space_constraint(a, VMEM) for a in args]
    return pl.pallas_call(
        kernel,
        out_shape=tuple(VMEM(shape, dtype) for shape, dtype in outs),
        in_specs=specs,
        out_specs=tuple(pl.BlockSpec(memory_space=VMEM) for _ in outs),
        scratch_shapes=scratch,
        compiler_params=pltpu.CompilerParams(vmem_limit_bytes=limit),
        cost_estimate=pl.CostEstimate(flops=flops, transcendentals=0, bytes_accessed=0) if flops else None,
        name=name,
    )(*args)


def in_hbm(*arrays):
    return [pltpu.with_memory_space_constraint(a, pltpu.MemorySpace.HBM) for a in arrays]


def pack_kernel(tok_ref, ids_ref, gw_ref, out_ref, meta_ref):
    rows, width = tok_ref.shape
    out_ref[:, :width] = tok_ref[...]
    w = gw_ref[...]
    high = w.astype(BF16).astype(F32)
    mid = (w - high).astype(BF16).astype(F32)
    meta_ref[...] = jnp.zeros(meta_ref.shape, F32)
    meta_ref[0:2, 0:rows] = ids_ref[...].astype(F32)
    meta_ref[2:4, 0:rows] = high
    meta_ref[4:6, 0:rows] = mid
    meta_ref[6:8, 0:rows] = w - high - mid
    out_ref[:, width:] = meta_ref[...].astype(BF16)


def packed(tokens, ids, gate_weights):
    rows, width = tokens.shape
    return pl.pallas_call(
        pack_kernel,
        out_shape=VMEM((rows, width + META), BF16),
        out_specs=pl.BlockSpec(memory_space=VMEM),
        scratch_shapes=[pltpu.VMEM((8, META), F32)],
        compiler_params=pltpu.CompilerParams(vmem_limit_bytes=2**20),
        cost_estimate=pl.CostEstimate(flops=2**35, transcendentals=0, bytes_accessed=0),
        name="pack",
    )(*in_hbm(tokens, ids.T, gate_weights.T))


def placement(meta, zh, block):
    rows = 8
    meta = meta.astype(F32)
    r = iota((X * 2 * SLOTS, rows), 0)
    expert = ((r // (2 * SLOTS)) * ZH + zh).astype(F32)
    named = jnp.where((meta[0:1, :rows] == expert) | (meta[1:2, :rows] == expert), 1.0, 0.0)
    before = jnp.where(iota((rows, rows), 0) < iota((rows, rows), 1), 1.0, 0.0)
    rank = dot(named.astype(BF16), before.astype(BF16))
    mine = (r // SLOTS) % 2 == block
    return jnp.where(mine & (named > 0.5) & (rank == (r % SLOTS).astype(F32)), 1.0, 0.0).astype(BF16)


def place_kernel(zh_ref, own_ref, halves_ref, out_ref, both_ref):
    width = out_ref.shape[-1]
    zh = zh_ref[0]
    both_ref[0:8] = own_ref[:, :width]
    both_ref[8:16] = halves_ref[1 - zh, :, :width]
    places = [placement(own_ref[:, width:], zh, 0), placement(halves_ref[1 - zh, :, width:], zh, 1)]
    slots = dot(jnp.concatenate(places, axis=1), both_ref[...]).astype(BF16)
    for x in range(X):
        for y in range(Y):
            out_ref[x * Y + y] = slots[x * 2 * SLOTS : (x + 1) * 2 * SLOTS]


def placed(zh, own, halves):
    width = own.shape[1] - META
    outs = [((X * Y, 2 * SLOTS, width), BF16)]
    return call(place_kernel, outs, (zh, own, halves), "place", [pltpu.VMEM((16, width), BF16)])[0]


BLOCK = 512


def hidden_units(rows, wg_ref, wu_ref, out_ref):
    for start in range(0, out_ref.shape[1], BLOCK):
        gate = dot(rows, wg_ref[0, :, start : start + BLOCK])
        up = dot(rows, wu_ref[0, :, start : start + BLOCK])
        out_ref[:, start : start + BLOCK] = (gate / (1.0 + jnp.exp(-gate)) * up).astype(BF16)


def down(hidden, wd_ref, out_ref):
    for start in range(0, out_ref.shape[1], BLOCK):
        out_ref[:, start : start + BLOCK] = dot(hidden, wd_ref[0, :, start : start + BLOCK]).astype(out_ref.dtype)


def hidden_kernel(rows_ref, wg_ref, wu_ref, out_ref):
    hidden_units(rows_ref[...], wg_ref, wu_ref, out_ref)


def down_kernel(hidden_ref, wd_ref, out_ref):
    down(hidden_ref[...], wd_ref, out_ref)


def expert_kernel(rows_ref, wg_ref, wu_ref, wd_ref, out_ref, hidden_ref):
    hidden_units(rows_ref[...], wg_ref, wu_ref, hidden_ref)
    down(hidden_ref[...], wd_ref, out_ref)


def mixing(meta, zh, block):
    rows = 8
    eye = jnp.where(iota((8, 8), 0) == iota((8, 8), 1), 1.0, 0.0).astype(BF16)
    fields = dot(eye, meta[:, :rows], ((1,), (1,)))
    lanes = X * Y * 2 * SLOTS
    r = iota((rows, lanes), 1)
    expert = ((r // (Y * 2 * SLOTS)) * ZH + zh).astype(F32)
    first = fields[:, 0:1] == expert
    second = fields[:, 1:2] == expert
    named = jnp.where(first | second, 1.0, 0.0)
    before = jnp.where(iota((rows, rows), 1) < iota((rows, rows), 0), 1.0, 0.0)
    rank = dot(before.astype(BF16), named.astype(BF16))
    w0 = fields[:, 2:3] + fields[:, 4:5] + fields[:, 6:7]
    w1 = fields[:, 3:4] + fields[:, 5:6] + fields[:, 7:8]
    mine = (r // SLOTS) % 2 == block
    weight = jnp.where(first, w0, jnp.where(second, w1, 0.0))
    return jnp.where(mine & (rank == (r % SLOTS).astype(F32)), weight, 0.0)


def split(weights):
    high = weights.astype(BF16).astype(F32)
    mid = (weights - high).astype(BF16).astype(F32)
    return jnp.concatenate([high, mid, weights - high - mid], axis=0).astype(BF16)


def weights_kernel(zh_ref, own_ref, halves_ref, own_out, other_out):
    width = own_ref.shape[1] - META
    own_out[...] = split(mixing(own_ref[:, width:], zh_ref[0], 0))
    other_out[...] = split(mixing(halves_ref[1 - zh_ref[0], :, width:], zh_ref[0], 1))


def both_kernel(own_ref, other_ref, rows_ref, keep_ref, send_ref):
    total = dot(jnp.concatenate([own_ref[...], other_ref[...]], axis=0), rows_ref[...])
    keep_ref[...] = total[0:8] + total[8:16] + total[16:24]
    send_ref[...] = (total[24:32] + total[32:40] + total[40:48]).astype(BF16)


def final_kernel(zh_ref, keep_ref, gathered_ref, out_ref):
    out_ref[...] = (keep_ref[...] + gathered_ref[1 - zh_ref[0]].astype(F32)).astype(BF16)


def swapped(value, axis):
    return lax.ppermute(value, axis, [(0, 1), (1, 0)])


def on_device(tokens, expert_ids, gate_weights, gate_proj, up_proj, down_proj):
    width = tokens.shape[1]
    units = gate_proj.shape[2]
    zh = lax.axis_index("zh").astype(jnp.int32).reshape(1)
    own = packed(tokens, expert_ids, gate_weights)
    halves = lax.all_gather(own, "zh")
    wg, wu, wd = gate_proj, up_proj, down_proj
    slots = placed(zh, own, halves)
    half = slots.shape[0] * slots.shape[1]
    rows = lax.all_to_all(slots, ("x", "y"), 0, 0, tiled=True).reshape(half, width)
    core_rows = swapped(rows, "core")
    third = 2 * half * width * units
    hidden = call(hidden_kernel, [((half, units), BF16)], (rows, wg, wu), "hidden", flops=2 * third)[0]
    core_rows, hidden = lax.optimization_barrier((core_rows, hidden))
    scratch = [pltpu.VMEM((half, units), BF16)]
    core_part = call(expert_kernel, [((half, width), BF16)], (core_rows, wg, wu, wd), "expert", scratch, flops=3 * third)[0]
    core_part, own, halves = lax.optimization_barrier((core_part, own, halves))
    arrived = swapped(core_part, "core")
    part = call(down_kernel, [((half, width), F32)], (hidden, wd), "down", flops=third)[0]
    outs = [((24, half), BF16), ((24, half), BF16)]
    mixers = call(weights_kernel, outs, (zh, own, halves), "weights", flops=2**28)
    arrived, part, (own_weights, other_weights) = lax.optimization_barrier((arrived, part, mixers))
    pair = (part + arrived.astype(F32)).astype(BF16).reshape(slots.shape)
    back = lax.all_to_all(pair, ("x", "y"), 0, 0, tiled=True)
    outs = [((8, width), F32), ((8, width), BF16)]
    keep, send = call(both_kernel, outs, (own_weights, other_weights, back.reshape(half, width)), "mix")
    gathered = lax.all_gather(send, "zh")
    return pl.pallas_call(
        final_kernel,
        out_shape=jax.ShapeDtypeStruct((8, width), BF16),
        in_specs=[pl.BlockSpec(memory_space=SMEM), pl.BlockSpec(memory_space=VMEM), pl.BlockSpec(memory_space=VMEM)],
        out_specs=pl.BlockSpec(memory_space=VMEM),
        compiler_params=pltpu.CompilerParams(vmem_limit_bytes=2**20),
        name="final",
    )(zh, pltpu.with_memory_space_constraint(keep, VMEM), pltpu.with_memory_space_constraint(gathered, VMEM))


def solution(mesh):
    dp = mesh.shape["dp"]
    fine = Mesh(mesh.devices.reshape(dp, X, ZH, Y, CORE), ("dp", "x", "zh", "y", "core"))
    every = P(("dp", "x", "zh", "y", "core"), None)
    return jax.shard_map(
        on_device,
        mesh=fine,
        in_specs=(
            every,
            every,
            every,
            P(("x", "zh"), None, ("y", "core")),
            P(("x", "zh"), None, ("y", "core")),
            P(("x", "zh"), ("y", "core"), None),
        ),
        out_specs=every,
        check_vma=False,
    )
```

```python
import functools

import jax
import jax.numpy as jnp
from jax import lax
from jax.experimental import pallas as pl
from jax.experimental.pallas import tpu as pltpu
from jax.sharding import Mesh, PartitionSpec as P

X, ZH, Y, CORE = 4, 2, 4, 2
SLOTS = 4
META = 128
BF16, F32 = jnp.bfloat16, jnp.float32
VMEM = pltpu.MemorySpace.VMEM
SMEM = pltpu.MemorySpace.SMEM


def dot(a, b, contract=((1,), (0,))):
    return lax.dot_general(a, b, (contract, ((), ())), preferred_element_type=F32)


def iota(shape, dim):
    return lax.broadcasted_iota(jnp.int32, shape, dim)


def call(kernel, outs, args, name, scratch=(), limit=8 * 2**20, flops=0):
    specs = [pl.BlockSpec(memory_space=SMEM if a.size == 1 else VMEM) for a in args]
    args = [a if a.size == 1 else pltpu.with_memory_space_constraint(a, VMEM) for a in args]
    return pl.pallas_call(
        kernel,
        out_shape=tuple(VMEM(shape, dtype) for shape, dtype in outs),
        in_specs=specs,
        out_specs=tuple(pl.BlockSpec(memory_space=VMEM) for _ in outs),
        scratch_shapes=scratch,
        compiler_params=pltpu.CompilerParams(vmem_limit_bytes=limit),
        cost_estimate=pl.CostEstimate(flops=flops, transcendentals=0, bytes_accessed=0) if flops else None,
        name=name,
    )(*args)


def in_hbm(*arrays):
    return [pltpu.with_memory_space_constraint(a, pltpu.MemorySpace.HBM) for a in arrays]


def pack_kernel(tok_ref, ids_ref, gw_ref, out_ref, meta_ref):
    rows, width = tok_ref.shape
    out_ref[:, :width] = tok_ref[...]
    w = gw_ref[...]
    high = w.astype(BF16).astype(F32)
    mid = (w - high).astype(BF16).astype(F32)
    meta_ref[...] = jnp.zeros(meta_ref.shape, F32)
    meta_ref[0:2, 0:rows] = ids_ref[...].astype(F32)
    meta_ref[2:4, 0:rows] = high
    meta_ref[4:6, 0:rows] = mid
    meta_ref[6:8, 0:rows] = w - high - mid
    out_ref[:, width:] = meta_ref[...].astype(BF16)


def packed(tokens, ids, gate_weights):
    rows, width = tokens.shape
    return pl.pallas_call(
        pack_kernel,
        out_shape=VMEM((rows, width + META), BF16),
        out_specs=pl.BlockSpec(memory_space=VMEM),
        scratch_shapes=[pltpu.VMEM((8, META), F32)],
        compiler_params=pltpu.CompilerParams(vmem_limit_bytes=2**20),
        name="pack",
    )(*in_hbm(tokens, ids.T, gate_weights.T))


def placement(meta, zh, block):
    rows = 8
    meta = meta.astype(F32)
    r = iota((X * 2 * SLOTS, rows), 0)
    expert = ((r // (2 * SLOTS)) * ZH + zh).astype(F32)
    named = jnp.where((meta[0:1, :rows] == expert) | (meta[1:2, :rows] == expert), 1.0, 0.0)
    before = jnp.where(iota((rows, rows), 0) < iota((rows, rows), 1), 1.0, 0.0)
    rank = dot(named.astype(BF16), before.astype(BF16))
    mine = (r // SLOTS) % 2 == block
    return jnp.where(mine & (named > 0.5) & (rank == (r % SLOTS).astype(F32)), 1.0, 0.0).astype(BF16)


def place_kernel(zh_ref, own_ref, halves_ref, out_ref, both_ref):
    width = out_ref.shape[-1]
    zh = zh_ref[0]
    both_ref[0:8] = own_ref[:, :width]
    both_ref[8:16] = halves_ref[1 - zh, :, :width]
    places = [placement(own_ref[:, width:], zh, 0), placement(halves_ref[1 - zh, :, width:], zh, 1)]
    slots = dot(jnp.concatenate(places, axis=1), both_ref[...]).astype(BF16)
    for x in range(X):
        for y in range(Y):
            out_ref[y * X + x] = slots[x * 2 * SLOTS : (x + 1) * 2 * SLOTS]


def placed(zh, own, halves):
    width = own.shape[1] - META
    outs = [((X * Y, 2 * SLOTS, width), BF16)]
    return call(place_kernel, outs, (zh, own, halves), "place", [pltpu.VMEM((16, width), BF16)], flops=2**35)[0]


BLOCK = 512


def hidden_units(rows, wg_ref, wu_ref, out_ref):
    for start in range(0, out_ref.shape[1], BLOCK):
        gate = dot(rows, wg_ref[0, :, start : start + BLOCK])
        up = dot(rows, wu_ref[0, :, start : start + BLOCK])
        out_ref[:, start : start + BLOCK] = (gate / (1.0 + jnp.exp(-gate)) * up).astype(BF16)


def down(hidden, wd_ref, out_ref):
    for start in range(0, out_ref.shape[1], BLOCK):
        out_ref[:, start : start + BLOCK] = dot(hidden, wd_ref[0, :, start : start + BLOCK]).astype(out_ref.dtype)


def hidden_kernel(rows_ref, wg_ref, wu_ref, out_ref):
    hidden_units(rows_ref[...], wg_ref, wu_ref, out_ref)


def down_kernel(hidden_ref, wd_ref, out_ref):
    down(hidden_ref[...], wd_ref, out_ref)


def expert_kernel(rows_ref, wg_ref, wu_ref, wd_ref, out_ref, hidden_ref):
    hidden_units(rows_ref[...], wg_ref, wu_ref, hidden_ref)
    down(hidden_ref[...], wd_ref, out_ref)


def mixing(meta, zh, block):
    rows = 8
    eye = jnp.where(iota((8, 8), 0) == iota((8, 8), 1), 1.0, 0.0).astype(BF16)
    fields = dot(eye, meta[:, :rows], ((1,), (1,)))
    lanes = X * Y * 2 * SLOTS
    r = iota((rows, lanes), 1)
    expert = (((r // (2 * SLOTS)) % X) * ZH + zh).astype(F32)
    first = fields[:, 0:1] == expert
    second = fields[:, 1:2] == expert
    named = jnp.where(first | second, 1.0, 0.0)
    before = jnp.where(iota((rows, rows), 1) < iota((rows, rows), 0), 1.0, 0.0)
    rank = dot(before.astype(BF16), named.astype(BF16))
    w0 = fields[:, 2:3] + fields[:, 4:5] + fields[:, 6:7]
    w1 = fields[:, 3:4] + fields[:, 5:6] + fields[:, 7:8]
    mine = (r // SLOTS) % 2 == block
    weight = jnp.where(first, w0, jnp.where(second, w1, 0.0))
    return jnp.where(mine & (rank == (r % SLOTS).astype(F32)), weight, 0.0)


def split(weights):
    high = weights.astype(BF16).astype(F32)
    mid = (weights - high).astype(BF16).astype(F32)
    return jnp.concatenate([high, mid, weights - high - mid], axis=0).astype(BF16)


def weights_kernel(zh_ref, own_ref, halves_ref, own_out, other_out):
    width = own_ref.shape[1] - META
    own_out[...] = split(mixing(own_ref[:, width:], zh_ref[0], 0))
    other_out[...] = split(mixing(halves_ref[1 - zh_ref[0], :, width:], zh_ref[0], 1))


def both_kernel(own_ref, other_ref, rows_ref, keep_ref, send_ref):
    total = dot(jnp.concatenate([own_ref[...], other_ref[...]], axis=0), rows_ref[...])
    keep_ref[...] = total[0:8] + total[8:16] + total[16:24]
    send_ref[...] = (total[24:32] + total[32:40] + total[40:48]).astype(BF16)


def final_kernel(zh_ref, keep_ref, gathered_ref, out_ref):
    out_ref[...] = (keep_ref[...] + gathered_ref[1 - zh_ref[0]].astype(F32)).astype(BF16)


def swapped(value, axis):
    return lax.ppermute(value, axis, [(0, 1), (1, 0)])


def on_device(tokens, expert_ids, gate_weights, gate_proj, up_proj, down_proj):
    width = tokens.shape[1]
    units = gate_proj.shape[2]
    zh = lax.axis_index("zh").astype(jnp.int32).reshape(1)
    own = packed(tokens, expert_ids, gate_weights)
    halves = lax.all_gather(own, "zh")
    wg, wu, wd = gate_proj, up_proj, down_proj
    slots = placed(zh, own, halves)
    half = slots.shape[0] * slots.shape[1]
    rows = lax.all_to_all(slots, ("y", "x"), 0, 0, tiled=True).reshape(half, width)
    core_rows = swapped(rows, "core")
    third = 2 * half * width * units
    hidden = call(hidden_kernel, [((half, units), BF16)], (rows, wg, wu), "hidden", flops=2 * third)[0]
    core_rows, hidden = lax.optimization_barrier((core_rows, hidden))
    scratch = [pltpu.VMEM((half, units), BF16)]
    core_part = call(expert_kernel, [((half, width), BF16)], (core_rows, wg, wu, wd), "expert", scratch, flops=3 * third)[0]
    core_part, own, halves = lax.optimization_barrier((core_part, own, halves))
    arrived = swapped(core_part, "core")
    part = call(down_kernel, [((half, width), F32)], (hidden, wd), "down", flops=third)[0]
    outs = [((24, half), BF16), ((24, half), BF16)]
    mixers = call(weights_kernel, outs, (zh, own, halves), "weights", flops=2**28)
    arrived, part, (own_weights, other_weights) = lax.optimization_barrier((arrived, part, mixers))
    pair = (part + arrived.astype(F32)).astype(BF16).reshape(slots.shape)
    back = lax.all_to_all(pair, ("y", "x"), 0, 0, tiled=True)
    outs = [((8, width), F32), ((8, width), BF16)]
    keep, send = call(both_kernel, outs, (own_weights, other_weights, back.reshape(half, width)), "mix")
    gathered = lax.all_gather(send, "zh")
    return pl.pallas_call(
        final_kernel,
        out_shape=jax.ShapeDtypeStruct((8, width), BF16),
        in_specs=[pl.BlockSpec(memory_space=SMEM), pl.BlockSpec(memory_space=VMEM), pl.BlockSpec(memory_space=VMEM)],
        out_specs=pl.BlockSpec(memory_space=VMEM),
        compiler_params=pltpu.CompilerParams(vmem_limit_bytes=2**20),
        name="final",
    )(zh, pltpu.with_memory_space_constraint(keep, VMEM), pltpu.with_memory_space_constraint(gathered, VMEM))


def solution(mesh):
    dp = mesh.shape["dp"]
    fine = Mesh(mesh.devices.reshape(dp, X, ZH, Y, CORE), ("dp", "x", "zh", "y", "core"))
    every = P(("dp", "x", "zh", "y", "core"), None)
    return jax.shard_map(
        on_device,
        mesh=fine,
        in_specs=(
            every,
            every,
            every,
            P(("x", "zh"), None, ("y", "core")),
            P(("x", "zh"), None, ("y", "core")),
            P(("x", "zh"), ("y", "core"), None),
        ),
        out_specs=every,
        check_vma=False,
    )
```

```python
import functools

import jax
import jax.numpy as jnp
from jax import lax
from jax.experimental import pallas as pl
from jax.experimental.pallas import tpu as pltpu
from jax.sharding import Mesh, PartitionSpec as P

X, ZH, Y, CORE = 4, 2, 4, 2
SLOTS = 4
META = 128
BF16, F32 = jnp.bfloat16, jnp.float32
VMEM = pltpu.MemorySpace.VMEM
SMEM = pltpu.MemorySpace.SMEM


def dot(a, b, contract=((1,), (0,))):
    return lax.dot_general(a, b, (contract, ((), ())), preferred_element_type=F32)


def iota(shape, dim):
    return lax.broadcasted_iota(jnp.int32, shape, dim)


def call(kernel, outs, args, name, scratch=(), limit=8 * 2**20, flops=0):
    specs = [pl.BlockSpec(memory_space=SMEM if a.size == 1 else VMEM) for a in args]
    args = [a if a.size == 1 else pltpu.with_memory_space_constraint(a, VMEM) for a in args]
    return pl.pallas_call(
        kernel,
        out_shape=tuple(VMEM(shape, dtype) for shape, dtype in outs),
        in_specs=specs,
        out_specs=tuple(pl.BlockSpec(memory_space=VMEM) for _ in outs),
        scratch_shapes=scratch,
        compiler_params=pltpu.CompilerParams(vmem_limit_bytes=limit),
        cost_estimate=pl.CostEstimate(flops=flops, transcendentals=0, bytes_accessed=0) if flops else None,
        name=name,
    )(*args)


def in_hbm(*arrays):
    return [pltpu.with_memory_space_constraint(a, pltpu.MemorySpace.HBM) for a in arrays]


def pack_kernel(tok_ref, ids_ref, gw_ref, out_ref, meta_ref):
    rows, width = tok_ref.shape
    out_ref[:, :width] = tok_ref[...]
    w = gw_ref[...]
    high = w.astype(BF16).astype(F32)
    mid = (w - high).astype(BF16).astype(F32)
    meta_ref[...] = jnp.zeros(meta_ref.shape, F32)
    meta_ref[0:2, 0:rows] = ids_ref[...].astype(F32)
    meta_ref[2:4, 0:rows] = high
    meta_ref[4:6, 0:rows] = mid
    meta_ref[6:8, 0:rows] = w - high - mid
    out_ref[:, width:] = meta_ref[...].astype(BF16)


def packed(tokens, ids, gate_weights):
    rows, width = tokens.shape
    return pl.pallas_call(
        pack_kernel,
        out_shape=VMEM((rows, width + META), BF16),
        out_specs=pl.BlockSpec(memory_space=VMEM),
        scratch_shapes=[pltpu.VMEM((8, META), F32)],
        compiler_params=pltpu.CompilerParams(vmem_limit_bytes=2**20),
        name="pack",
    )(*in_hbm(tokens, ids.T, gate_weights.T))


def placement(meta, zh, block):
    rows = 8
    meta = meta.astype(F32)
    r = iota((X * 2 * SLOTS, rows), 0)
    expert = ((r // (2 * SLOTS)) * ZH + zh).astype(F32)
    named = jnp.where((meta[0:1, :rows] == expert) | (meta[1:2, :rows] == expert), 1.0, 0.0)
    before = jnp.where(iota((rows, rows), 0) < iota((rows, rows), 1), 1.0, 0.0)
    rank = dot(named.astype(BF16), before.astype(BF16))
    mine = (r // SLOTS) % 2 == block
    return jnp.where(mine & (named > 0.5) & (rank == (r % SLOTS).astype(F32)), 1.0, 0.0).astype(BF16)


def place_kernel(zh_ref, own_ref, halves_ref, out_ref, both_ref):
    width = out_ref.shape[-1]
    zh = zh_ref[0]
    both_ref[0:8] = own_ref[:, :width]
    both_ref[8:16] = halves_ref[1 - zh, :, :width]
    places = [placement(own_ref[:, width:], zh, 0), placement(halves_ref[1 - zh, :, width:], zh, 1)]
    slots = dot(jnp.concatenate(places, axis=1), both_ref[...]).astype(BF16)
    for x in range(X):
        for y in range(Y):
            out_ref[x * Y + y] = slots[x * 2 * SLOTS : (x + 1) * 2 * SLOTS]


def placed(zh, own, halves):
    width = own.shape[1] - META
    outs = [((X * Y, 2 * SLOTS, width), BF16)]
    return call(place_kernel, outs, (zh, own, halves), "place", [pltpu.VMEM((16, width), BF16)], flops=2**35)[0]


BLOCK = 512


def hidden_units(rows, wg_ref, wu_ref, out_ref):
    for start in range(0, out_ref.shape[1], BLOCK):
        gate = dot(rows, wg_ref[0, :, start : start + BLOCK])
        up = dot(rows, wu_ref[0, :, start : start + BLOCK])
        out_ref[:, start : start + BLOCK] = (gate / (1.0 + jnp.exp(-gate)) * up).astype(BF16)


def down(hidden, wd_ref, out_ref):
    for start in range(0, out_ref.shape[1], BLOCK):
        out_ref[:, start : start + BLOCK] = dot(hidden, wd_ref[0, :, start : start + BLOCK]).astype(out_ref.dtype)


def hidden_kernel(rows_ref, wg_ref, wu_ref, out_ref):
    hidden_units(rows_ref[...], wg_ref, wu_ref, out_ref)


def down_kernel(hidden_ref, wd_ref, out_ref):
    down(hidden_ref[...], wd_ref, out_ref)


def expert_kernel(rows_ref, wg_ref, wu_ref, wd_ref, out_ref, hidden_ref):
    hidden_units(rows_ref[...], wg_ref, wu_ref, hidden_ref)
    down(hidden_ref[...], wd_ref, out_ref)


def mixing(meta, zh, block):
    rows = 8
    eye = jnp.where(iota((8, 8), 0) == iota((8, 8), 1), 1.0, 0.0).astype(BF16)
    fields = dot(eye, meta[:, :rows], ((1,), (1,)))
    lanes = X * Y * 2 * SLOTS
    r = iota((rows, lanes), 1)
    expert = ((r // (Y * 2 * SLOTS)) * ZH + zh).astype(F32)
    first = fields[:, 0:1] == expert
    second = fields[:, 1:2] == expert
    named = jnp.where(first | second, 1.0, 0.0)
    before = jnp.where(iota((rows, rows), 1) < iota((rows, rows), 0), 1.0, 0.0)
    rank = dot(before.astype(BF16), named.astype(BF16))
    w0 = fields[:, 2:3] + fields[:, 4:5] + fields[:, 6:7]
    w1 = fields[:, 3:4] + fields[:, 5:6] + fields[:, 7:8]
    mine = (r // SLOTS) % 2 == block
    weight = jnp.where(first, w0, jnp.where(second, w1, 0.0))
    return jnp.where(mine & (rank == (r % SLOTS).astype(F32)), weight, 0.0)


def split(weights):
    high = weights.astype(BF16).astype(F32)
    mid = (weights - high).astype(BF16).astype(F32)
    return jnp.concatenate([high, mid, weights - high - mid], axis=0).astype(BF16)


def weights_kernel(zh_ref, own_ref, halves_ref, own_out, other_out):
    width = own_ref.shape[1] - META
    own_out[...] = split(mixing(own_ref[:, width:], zh_ref[0], 0))
    other_out[...] = split(mixing(halves_ref[1 - zh_ref[0], :, width:], zh_ref[0], 1))


def both_kernel(own_ref, other_ref, rows_ref, keep_ref, send_ref):
    total = dot(jnp.concatenate([own_ref[...], other_ref[...]], axis=0), rows_ref[...])
    keep_ref[...] = total[0:8] + total[8:16] + total[16:24]
    send_ref[...] = (total[24:32] + total[32:40] + total[40:48]).astype(BF16)


def swapped(value, axis):
    return lax.ppermute(value, axis, [(0, 1), (1, 0)])


def on_device(tokens, expert_ids, gate_weights, gate_proj, up_proj, down_proj):
    width = tokens.shape[1]
    units = gate_proj.shape[2]
    zh = lax.axis_index("zh").astype(jnp.int32).reshape(1)
    own = packed(tokens, expert_ids, gate_weights)
    halves = lax.all_gather(own, "zh")
    wg, wu, wd = gate_proj, up_proj, down_proj
    slots = placed(zh, own, halves)
    half = slots.shape[0] * slots.shape[1]
    rows = lax.all_to_all(slots, ("x", "y"), 0, 0, tiled=True).reshape(half, width)
    core_rows = swapped(rows, "core")
    third = 2 * half * width * units
    hidden = call(hidden_kernel, [((half, units), BF16)], (rows, wg, wu), "hidden", flops=2 * third)[0]
    core_rows, hidden = lax.optimization_barrier((core_rows, hidden))
    scratch = [pltpu.VMEM((half, units), BF16)]
    core_part = call(expert_kernel, [((half, width), BF16)], (core_rows, wg, wu, wd), "expert", scratch, flops=3 * third)[0]
    core_part, own, halves = lax.optimization_barrier((core_part, own, halves))
    arrived = swapped(core_part, "core")
    part = call(down_kernel, [((half, width), F32)], (hidden, wd), "down", flops=third)[0]
    outs = [((24, half), BF16), ((24, half), BF16)]
    mixers = call(weights_kernel, outs, (zh, own, halves), "weights", flops=2**28)
    arrived, part, (own_weights, other_weights) = lax.optimization_barrier((arrived, part, mixers))
    pair = (part + arrived.astype(F32)).astype(BF16).reshape(slots.shape)
    back = lax.all_to_all(pair, ("x", "y"), 0, 0, tiled=True)
    outs = [((8, width), F32), ((8, width), BF16)]
    keep, send = call(both_kernel, outs, (own_weights, other_weights, back.reshape(half, width)), "mix")
    gathered = lax.all_gather(send, "zh")
    arriving = jnp.where(zh[0] == 0, gathered[1], gathered[0])
    return (keep + arriving.astype(F32)).astype(BF16)


def solution(mesh):
    dp = mesh.shape["dp"]
    fine = Mesh(mesh.devices.reshape(dp, X, ZH, Y, CORE), ("dp", "x", "zh", "y", "core"))
    every = P(("dp", "x", "zh", "y", "core"), None)
    return jax.shard_map(
        on_device,
        mesh=fine,
        in_specs=(
            every,
            every,
            every,
            P(("x", "zh"), None, ("y", "core")),
            P(("x", "zh"), None, ("y", "core")),
            P(("x", "zh"), ("y", "core"), None),
        ),
        out_specs=every,
        check_vma=False,
    )
```
